32 devices in a mesh: groups: 2 (over x), out: 16 (over z, y, core).
Axes of the slice: x: 2, y: 2, z: 4, core: 2. Of those that a mesh axis runs over, the one named last changes fastest.
Arguments:
- stream: bfloat16 [128, 12288], P('groups', 'out'), parts along dimension 0, may hold values from -6 to 6
- norm_gain: float32 [12288], replicated, may hold values from 0.5 to 1.5
- w_query: bfloat16 [12288, 6144], P(None, 'out')
- w_keyval: bfloat16 [12288, 1024], P(None, 'out'), may hold values from -0.0546875 to 0.0546875
- w_out: bfloat16 [6144, 12288], P('out'), may hold values from -0.75 to 0.75
- lengths: int32 [128], P(('groups', 'out')), parts along dimension 0, may hold values from 1 to 512, as said below
- key_cache: bfloat16 [128, 512, 512], P(('groups', 'out')), parts along dimension 0, may hold values from -127 to 127, as said below
- value_cache: bfloat16 [128, 512, 512], P(('groups', 'out')), parts along dimension 0, may hold values from -127 to 127, as said below
- key_scales: int32 [128, 4, 4], P(('groups', 'out')), parts along dimension 0, may hold values from -8 to -6
- value_scales: int32 [128, 4, 4], P(('groups', 'out')), parts along dimension 0, may hold values from -8 to -6
Outputs:
- new_stream: bfloat16 [128, 12288], P('groups', 'out'), parts along dimension 0
The draws below stay inside these ranges and needn't reach their ends.
There are 2 independent parts, one for each index of `groups`. The reference program is written for one: setup_inputs(seed, part) draws one part's arguments, and reference() takes and returns one part's arrays. A program takes and returns all parts, laid end to end along the dimension named above; an argument that names none is the same for every part. Nothing has to cross between parts.
Inputs may be any that keep to these rules, and one draw needn't show every extreme that they name: `lengths`: every row holds at least one earlier token; in every draw some row holds exactly 512. `key_cache`: whole numbers, codes of an eight-bit cache. `value_cache`: whole numbers, codes of an eight-bit cache.
All inputs are finite; a program needn't handle non-finite values.
Results may differ from the reference program's by a relative error of at most 0.024.
The reference program's roundings to bfloat16 on the way count: a program that leaves them out, or rounds other values in their place, can miss the bound.
Values may be sent and summed in bfloat16 or wider, within the bound.
No kernel may reach another device: no remote copies, remote signals or barrier semaphores. Data moves between devices by JAX's collectives and lax.ppermute only.
A program may use at most 64 MiB of HBM per device.

```python
import math
import jax
import jax.numpy as jnp
from jax import lax

D = 12288
HQ = 48
KVH = 4
HD = 128
CAP = 512
ROWS = 64
GRP = 12
NB = 4


def draw_lengths(key, part):
    first, second, third = jax.random.split(key, 3)
    base = jax.random.randint(first, (ROWS,), 1, CAP + 1)
    coin = jax.random.randint(second, (ROWS,), 0, 4)
    lens = jnp.where(coin == 0, base, base // 4 + 1)
    chosen = jax.random.randint(third, (), 0, ROWS)
    lens = jnp.where(jnp.arange(ROWS) == chosen, CAP, lens)
    return lens.astype(jnp.int32)


def draw_codes(key):
    first = jax.random.fold_in(key, 0)
    codes = jax.random.randint(first, (ROWS, CAP, KVH * HD), -127, 128)
    return codes.astype(jnp.float32).astype(jnp.bfloat16)


def draw_key_cache(key, part):
    return draw_codes(jax.random.fold_in(key, 11))


def draw_value_cache(key, part):
    return draw_codes(jax.random.fold_in(key, 23))


def draw_w_query(key, part):
    first, second, third, fourth = jax.random.split(jax.random.fold_in(key, 37), 4)
    base = jax.random.truncated_normal(first, -4.0, 4.0, (D, HQ * HD), jnp.float32)
    strength = jax.random.uniform(third, (HQ,), jnp.float32, 48.0, 96.0)
    coin = jax.random.randint(second, (HQ,), 0, 6)
    forced = jax.random.randint(fourth, (), 0, HQ)
    heads = jnp.arange(HQ)
    boosted = jnp.logical_or(coin == 0, heads == forced)
    factor = jnp.where(boosted, strength, 1.0)
    column_factor = jnp.repeat(factor, HD)
    return (base * column_factor[None, :] * D ** (-0.5)).astype(jnp.bfloat16)


def set_ends(drawn, own_key, least, largest):
    longest = drawn.shape.index(max(drawn.shape))
    spots = []
    for shift in (0, 1):
        where = [jax.random.randint(jax.random.fold_in(own_key, axis), (), 0, length) for axis, length in enumerate(drawn.shape)]
        where[longest] = (where[longest] + shift) % drawn.shape[longest]
        spots.append(tuple(where))
    return drawn.at[spots[0]].set(least).at[spots[1]].set(largest)


def with_spikes(values, own_key, source, target, parts, factor):
    def block_of(dim):
        return (jnp.arange(values.shape[dim]) // (values.shape[dim] // parts)).reshape((-1,) + (1,) * (values.ndim - 1 - dim))

    first = jax.random.permutation(own_key, parts)[block_of(target)]
    other_side = (block_of(target) + parts // 2) % parts
    return jnp.where((block_of(source) == first) | (block_of(source) == other_side), factor * values, values)


def steps_of(stream_key, shape, cuts, low, high):
    def one(dim, parts):
        draws = jax.random.uniform(jax.random.fold_in(jax.random.fold_in(stream_key, 6), dim), (parts,), jnp.float32, low / len(cuts), high / len(cuts))
        return jnp.repeat(jnp.exp(draws), shape[dim] // parts).reshape((-1,) + (1,) * (len(shape) - dim - 1))

    gain = one(*cuts[0])
    for cut in cuts[1:]:
        gain = gain * one(*cut)
    return gain


def normal_values(stream_key, extent, deviation, limit, cuts=(), held_as=jnp.bfloat16):
    level = steps_of(stream_key, extent, cuts, -0.22, 0.18) if cuts else 1.0
    entries = jax.random.normal(stream_key, extent, jnp.float32) * deviation * level
    return jnp.minimum(jnp.maximum(entries, -limit), limit).astype(held_as)


def gaussian_with(stream_key, extent, deviation, limit, shards, heavy, held_as=jnp.bfloat16):
    array = deviation * jax.random.normal(stream_key, extent, jnp.float32)
    if shards:
        array = array * steps_of(stream_key, extent, shards, -0.22, 0.18)
    return jnp.clip(with_spikes(array, jax.random.fold_in(stream_key, 3), *heavy), -limit, limit).astype(held_as)


def setup_inputs(seed: int = 0, part: int = 0) -> dict:
    splits = jax.random.split(jax.random.key(seed), 11)
    part_keys = jax.random.split(jax.random.fold_in(splits[10], part), 11)
    return {
        "stream": normal_values(part_keys[0], (ROWS, D), 1.0, 6.0, ((1, 16),)),
        "norm_gain": jnp.clip(1.0 + 0.1 * jax.random.normal(splits[1], (D,), jnp.float32), 0.5, 1.5),
        "w_query": draw_w_query(jax.random.fold_in(splits[10], 71), part),
        "w_keyval": normal_values(splits[3], (D, 2 * KVH * HD), D ** -0.5, 0.0546875, ((1, 16),)),
        "w_out": gaussian_with(splits[4], (HQ * HD, D), HD ** -0.5, 0.75, ((0, 16),), (0, 1, 16, 2.0)),
        "lengths": draw_lengths(jax.random.fold_in(jax.random.fold_in(splits[10], part), 71), part),
        "key_cache": draw_key_cache(jax.random.fold_in(jax.random.fold_in(splits[10], part), 71), part),
        "value_cache": draw_value_cache(jax.random.fold_in(jax.random.fold_in(splits[10], part), 71), part),
        "key_scales": set_ends(jax.random.randint(part_keys[8], (ROWS, NB, KVH), -8, -5), jax.random.fold_in(part_keys[8], 1), -8, (-5) - 1).astype(jnp.int32),
        "value_scales": set_ends(jax.random.randint(part_keys[9], (ROWS, NB, KVH), -8, -5), jax.random.fold_in(part_keys[9], 1), -8, (-5) - 1).astype(jnp.int32),
    }


rope_base = 1000000.0
norm_eps = 1e-05

def rotate(vec, position):
    half = vec.shape[-1] // 2
    index = jnp.arange(half, dtype=jnp.float32)
    freq = jnp.exp(index * (-2.0 * math.log(rope_base) / vec.shape[-1]))
    angle = position * freq
    cosine = jnp.cos(angle)
    sine = jnp.sin(angle)
    first = vec[..., :half]
    second = vec[..., half:]
    return jnp.concatenate([first * cosine - second * sine, second * cosine + first * sine], axis=-1)

def dequant(cache, scales):
    rows, span, width = cache.shape
    blocks = scales.shape[1]
    factor = jnp.exp2(scales.astype(jnp.float32)).astype(jnp.bfloat16)
    shaped = cache.reshape(rows, blocks, span // blocks, KVH, width // KVH)
    return (shaped * factor[:, :, None, :, None]).reshape(rows, span, KVH, width // KVH)

def reference(stream, norm_gain, w_query, w_keyval, w_out, lengths, key_cache, value_cache, key_scales, value_scales):
    xf = stream.astype(jnp.float32)
    meansq = lax.optimization_barrier(jnp.mean(xf * xf, axis=-1, keepdims=True))
    normed = (xf * lax.rsqrt(meansq + norm_eps) * norm_gain).astype(jnp.bfloat16)
    query = jnp.dot(normed, w_query, preferred_element_type=jnp.float32).astype(jnp.bfloat16)
    keyval = jnp.dot(normed, w_keyval, preferred_element_type=jnp.float32).astype(jnp.bfloat16)
    position = lengths.astype(jnp.float32)[:, None, None]
    rotated = rotate(query.astype(jnp.float32).reshape(ROWS, HQ, HD), position).astype(jnp.bfloat16)
    rotated = rotated.reshape(ROWS, KVH, GRP, HD).astype(jnp.float32)
    new_key = rotate(keyval[:, :KVH * HD].astype(jnp.float32).reshape(ROWS, KVH, HD), position).astype(jnp.bfloat16)
    new_value = keyval[:, KVH * HD:].reshape(ROWS, KVH, HD)
    keys = dequant(key_cache, key_scales).astype(jnp.float32)
    values = dequant(value_cache, value_scales).astype(jnp.float32)
    factor = HD ** (-0.5)
    scores = jnp.einsum('rkgd,rjkd->rkgj', rotated, keys) * factor
    valid = jnp.arange(CAP, dtype=jnp.int32)[None, :] < lengths[:, None]
    scores = jnp.where(valid[:, None, None, :], scores, -jnp.inf)
    own = jnp.einsum('rkgd,rkd->rkg', rotated, new_key.astype(jnp.float32)) * factor
    top = jnp.maximum(lax.optimization_barrier(jnp.max(scores, axis=-1)), own)
    weights = jnp.exp(scores - top[..., None])
    own_weight = jnp.exp(own - top)
    total = lax.optimization_barrier(jnp.sum(weights, axis=-1)) + own_weight
    rounded = weights.astype(jnp.bfloat16).astype(jnp.float32)
    own_rounded = lax.optimization_barrier(own_weight.astype(jnp.bfloat16)).astype(jnp.float32)
    summed = jnp.einsum('rkgj,rjkd->rkgd', rounded, values)
    summed = summed + own_rounded[..., None] * new_value.astype(jnp.float32)[:, :, None, :]
    attended = (summed / total[..., None]).astype(jnp.bfloat16).reshape(ROWS, HQ * HD)
    projected = jnp.dot(attended, w_out, preferred_element_type=jnp.float32)
    return (xf + projected).astype(jnp.bfloat16)
```

```python
import math

import jax
import jax.numpy as jnp
from jax import lax
from jax.experimental import pallas as pl
from jax.experimental.pallas import tpu as pltpu
from jax.sharding import PartitionSpec as P

HQ = 48
KVH = 4
HD = 128


rope_base = 1000000.0
norm_eps = 1e-05


def rotate(vec, position):
    half = vec.shape[-1] // 2
    index = jnp.arange(half, dtype=jnp.float32)
    freq = jnp.exp(index * (-2.0 * math.log(rope_base) / vec.shape[-1]))
    angle = position * freq
    cosine = jnp.cos(angle)
    sine = jnp.sin(angle)
    first = vec[..., :half]
    second = vec[..., half:]
    return jnp.concatenate(
        [first * cosine - second * sine, second * cosine + first * sine], axis=-1
    )


def dequant(cache, scales):
    rows, span, width = cache.shape
    blocks = scales.shape[1]
    factor = jnp.exp2(scales.astype(jnp.float32)).astype(jnp.bfloat16)
    shaped = cache.reshape(rows, blocks, span // blocks, KVH, width // KVH)
    return (shaped * factor[:, :, None, :, None]).reshape(rows, span, KVH, width // KVH)


def per_device_general(
    stream,
    norm_gain,
    w_query,
    w_keyval,
    w_out,
    lengths,
    key_cache,
    value_cache,
    key_scales,
    value_scales,
):
    local_rows = lengths.shape[0]
    xf = stream.astype(jnp.float32)
    whole = lax.all_gather(stream, "out", axis=1, tiled=True).astype(jnp.float32)
    meansq = jnp.mean(whole * whole, axis=-1, keepdims=True)
    normed = (whole * lax.rsqrt(meansq + norm_eps) * norm_gain).astype(jnp.bfloat16)
    q_local = jnp.dot(normed, w_query, preferred_element_type=jnp.float32).astype(jnp.bfloat16)
    kv_local = jnp.dot(normed, w_keyval, preferred_element_type=jnp.float32).astype(jnp.bfloat16)
    q_rows, kv_rows = (
        lax.all_to_all(q_local, "out", split_axis=0, concat_axis=1, tiled=True),
        lax.all_to_all(kv_local, "out", split_axis=0, concat_axis=1, tiled=True),
    )
    position = lengths.astype(jnp.float32)[:, None, None]
    rotated = rotate(q_rows.astype(jnp.float32).reshape(local_rows, HQ, HD), position).astype(
        jnp.bfloat16
    )
    rotated = rotated.reshape(local_rows, KVH, HQ // KVH, HD)
    new_key = rotate(
        kv_rows[:, : KVH * HD].astype(jnp.float32).reshape(local_rows, KVH, HD), position
    ).astype(jnp.bfloat16)
    new_value = kv_rows[:, KVH * HD :].reshape(local_rows, KVH, HD)
    factor = HD ** (-0.5)
    own = jnp.einsum("rkgd,rkd->rkg", rotated, new_key, preferred_element_type=jnp.float32) * factor
    span = key_cache.shape[1]
    scores = (
        jnp.einsum(
            "rkgd,rjkd->rkgj",
            rotated,
            dequant(key_cache, key_scales),
            preferred_element_type=jnp.float32,
        )
        * factor
    )
    valid = jnp.arange(span, dtype=jnp.int32)[None, :] < lengths[:, None]
    scores = jnp.where(valid[:, None, None, :], scores, -jnp.inf)
    top = jnp.maximum(jnp.max(scores, axis=-1), own)
    weights = jnp.exp(scores - top[..., None])
    own_weight = jnp.exp(own - top)
    total = jnp.sum(weights, axis=-1) + own_weight
    own_rounded = lax.optimization_barrier(own_weight.astype(jnp.bfloat16)).astype(jnp.float32)
    summed = jnp.einsum(
        "rkgj,rjkd->rkgd",
        weights.astype(jnp.bfloat16),
        dequant(value_cache, value_scales),
        preferred_element_type=jnp.float32,
    )
    summed = summed + own_rounded[..., None] * new_value.astype(jnp.float32)[:, :, None, :]
    attended = (summed / total[..., None]).astype(jnp.bfloat16).reshape(local_rows, HQ * HD)
    heads = lax.all_to_all(attended, "out", split_axis=1, concat_axis=0, tiled=True)
    partial_terms = jnp.dot(heads, w_out, preferred_element_type=jnp.float32)
    projected = lax.psum_scatter(partial_terms, "out", scatter_dimension=1, tiled=True)
    return (xf + projected).astype(jnp.bfloat16)


def swapped(value, bit, size):
    return lax.ppermute(value, "out", [(i, i ^ bit) for i in range(size)])


def project_kernel(order, pieces, me_ref, *refs):
    shards = refs[:pieces]
    gain_ref, wq_hbm, wkv_hbm, out_ref, wq_ref, wkv_ref, q_sem, kv_sem = refs[pieces:]
    rows, depth = shards[0].shape
    columns = wq_ref.shape[-1]
    me = me_ref[0]

    def owner(k):
        return lax.bitwise_xor(me, order[k])

    def q_copy(k):
        start = pl.multiple_of(owner(k) * depth, 128)
        return pltpu.make_async_copy(wq_hbm.at[pl.ds(start, depth)], wq_ref.at[k], q_sem.at[k])

    kv_copy = pltpu.make_async_copy(wkv_hbm, wkv_ref, kv_sem)
    for k in range(pieces):
        q_copy(k).start()
        if k == 0:
            kv_copy.start()
    square = jnp.zeros((rows, 128), jnp.float32)
    for k in range(pieces):
        part = shards[k][...].astype(jnp.float32)
        part = part * part
        for lane in range(0, depth, 128):
            square += part[:, lane : lane + 128]
    meansq = jnp.sum(square, axis=-1, keepdims=True) / (depth * pieces)
    inverse = lax.rsqrt(meansq + norm_eps)
    kv_copy.wait()
    q_sum = jnp.zeros((rows, columns), jnp.float32)
    kv_sum = jnp.zeros((rows, wkv_ref.shape[0]), jnp.float32)
    for k in range(pieces):
        gain = gain_ref[pl.ds(owner(k), 1), :]
        normed = (shards[k][...].astype(jnp.float32) * inverse * gain).astype(jnp.bfloat16)
        start = pl.multiple_of(owner(k) * depth, 128)
        kv_sum += lax.dot_general(
            normed,
            wkv_ref[:, pl.ds(start, depth)],
            (((1,), (1,)), ((), ())),
            preferred_element_type=jnp.float32,
        )
        q_copy(k).wait()
        q_sum += jnp.dot(normed, wq_ref[k], preferred_element_type=jnp.float32)
    out_ref[:, :columns] = q_sum.astype(jnp.bfloat16)
    out_ref[:, columns:] = kv_sum.astype(jnp.bfloat16)


def project(me, order, shards, norm_gain, w_query, w_keyval):
    pieces = len(shards)
    rows, depth = shards[0].shape
    columns, kv_columns = w_query.shape[1], w_keyval.shape[1]
    vmem = pl.BlockSpec(memory_space=pltpu.VMEM)
    hbm = pl.BlockSpec(memory_space=pl.ANY)
    return pl.pallas_call(
        lambda *refs: project_kernel(order, pieces, *refs),
        out_shape=jax.ShapeDtypeStruct((rows, columns + kv_columns), jnp.bfloat16),
        in_specs=[pl.BlockSpec(memory_space=pltpu.SMEM)] + [vmem] * (pieces + 1) + [hbm] * 2,
        out_specs=vmem,
        scratch_shapes=[
            pltpu.VMEM((pieces, depth, columns), jnp.bfloat16),
            pltpu.VMEM((kv_columns, pieces * depth), jnp.bfloat16),
            pltpu.SemaphoreType.DMA((pieces,)),
            pltpu.SemaphoreType.DMA,
        ],
        compiler_params=pltpu.CompilerParams(vmem_limit_bytes=24 * 1024 * 1024),
        name="project",
    )(me, *shards, norm_gain.reshape(pieces, depth), w_query, w_keyval.T)


def expand_kernel(order, me_ref, heads_ref, w_hbm, out_ref, w_ref, sem):
    width = out_ref.shape[-1]
    me = me_ref[0]

    def copy(k):
        start = pl.multiple_of(lax.bitwise_xor(me, order[k]) * width, 128)
        return pltpu.make_async_copy(w_hbm.at[:, pl.ds(start, width)], w_ref.at[k], sem.at[k])

    for k in range(len(order)):
        copy(k).start()
    heads = heads_ref[...]
    for k in range(len(order)):
        copy(k).wait()
        out_ref[k] = jnp.dot(heads, w_ref[k], preferred_element_type=jnp.float32).astype(out_ref.dtype)


def expand(me, order, heads, w_out, width, dtype):
    vmem = pl.BlockSpec(memory_space=pltpu.VMEM)
    return pl.pallas_call(
        lambda *refs: expand_kernel(order, *refs),
        out_shape=jax.ShapeDtypeStruct((len(order), heads.shape[0], width), dtype),
        in_specs=[pl.BlockSpec(memory_space=pltpu.SMEM), vmem, pl.BlockSpec(memory_space=pl.ANY)],
        out_specs=vmem,
        scratch_shapes=[
            pltpu.VMEM((len(order), w_out.shape[0], width), jnp.bfloat16),
            pltpu.SemaphoreType.DMA((len(order),)),
        ],
        compiler_params=pltpu.CompilerParams(vmem_limit_bytes=16 * 1024 * 1024),
        name="expand",
    )(me, heads, w_out)


def attend(q_rows, kv_rows, lengths, key_cache, value_cache, key_scales, value_scales):
    local_rows = lengths.shape[0]
    position = lengths.astype(jnp.float32)[:, None, None]
    rotated = rotate(q_rows.astype(jnp.float32).reshape(local_rows, HQ, HD), position).astype(
        jnp.bfloat16
    )
    rotated = rotated.reshape(local_rows, KVH, HQ // KVH, HD)
    new_key = rotate(
        kv_rows[:, : KVH * HD].astype(jnp.float32).reshape(local_rows, KVH, HD), position
    ).astype(jnp.bfloat16)
    new_value = kv_rows[:, KVH * HD :].reshape(local_rows, KVH, HD)
    factor = HD ** (-0.5)
    own = jnp.einsum("rkgd,rkd->rkg", rotated, new_key, preferred_element_type=jnp.float32) * factor
    span = key_cache.shape[1]
    scores = (
        jnp.einsum(
            "rkgd,rjkd->rkgj",
            rotated,
            dequant(key_cache, key_scales),
            preferred_element_type=jnp.float32,
        )
        * factor
    )
    valid = jnp.arange(span, dtype=jnp.int32)[None, :] < lengths[:, None]
    scores = jnp.where(valid[:, None, None, :], scores, -jnp.inf)
    top = jnp.maximum(jnp.max(scores, axis=-1), own)
    weights = jnp.exp(scores - top[..., None])
    own_weight = jnp.exp(own - top)
    total = jnp.sum(weights, axis=-1) + own_weight
    own_rounded = lax.optimization_barrier(own_weight.astype(jnp.bfloat16)).astype(jnp.float32)
    summed = jnp.einsum(
        "rkgj,rjkd->rkgd",
        weights.astype(jnp.bfloat16),
        dequant(value_cache, value_scales),
        preferred_element_type=jnp.float32,
    )
    summed = summed + own_rounded[..., None] * new_value.astype(jnp.float32)[:, :, None, :]
    return (summed / total[..., None]).astype(jnp.bfloat16).reshape(local_rows, HQ * HD)


def per_device(
    size,
    stream,
    norm_gain,
    w_query,
    w_keyval,
    w_out,
    lengths,
    key_cache,
    value_cache,
    key_scales,
    value_scales,
):
    local_rows = lengths.shape[0]
    me = lax.axis_index("out").astype(jnp.int32)[None]
    width = stream.shape[1]
    columns = w_query.shape[1]

    bits = [1 << k for k in reversed(range(size.bit_length() - 1))]
    held = {0: stream}
    for bit in bits:
        for mask in list(held):
            held[mask | bit] = swapped(held[mask], bit, size)
    order = list(held)
    qkv = project(me, order, [held[m] for m in order], norm_gain, w_query, w_keyval)

    rows = lax.all_to_all(
        qkv.reshape(size, local_rows, qkv.shape[1]), "out", split_axis=0, concat_axis=0, tiled=True
    )
    q_rows = jnp.swapaxes(rows[:, :, :columns], 0, 1).reshape(local_rows, size * columns)
    kv_rows = jnp.swapaxes(rows[:, :, columns:], 0, 1).reshape(local_rows, -1)
    attended = attend(
        q_rows, kv_rows, lengths, key_cache, value_cache, key_scales, value_scales
    )
    heads = lax.all_to_all(
        jnp.swapaxes(attended.reshape(local_rows, size, columns), 0, 1),
        "out",
        split_axis=0,
        concat_axis=0,
        tiled=True,
    ).reshape(size * local_rows, columns)

    away = [m for m in range(size - 1, -1, -1) if m & 1]
    near = [m ^ 1 for m in away]
    sent = swapped(expand(me, away, heads, w_out, width, jnp.bfloat16), 1, size)
    kept = expand(me, near, heads, w_out, width, jnp.float32)
    owed = {m: kept[k] + sent[k].astype(jnp.float32) for k, m in enumerate(near)}
    for bit in bits[-2::-1]:
        for mask in sorted((m for m in owed if m & bit), reverse=True):
            got = swapped(owed.pop(mask).astype(jnp.bfloat16), bit, size)
            owed[mask ^ bit] = owed[mask ^ bit] + got.astype(jnp.float32)
    return (stream.astype(jnp.float32) + owed[0]).astype(jnp.bfloat16)


def solution(mesh):
    size = mesh.shape["out"]

    def step(stream, *rest):
        if size & (size - 1) == 0 and stream.shape[1] % 128 == 0 and rest[1].shape[1] % HD == 0:
            return per_device(size, stream, *rest)
        return per_device_general(stream, *rest)

    return jax.shard_map(
        step,
        mesh=mesh,
        in_specs=(
            P("groups", "out"),
            P(),
            P(None, "out"),
            P(None, "out"),
            P("out", None),
            P(("groups", "out")),
            P(("groups", "out"), None, None),
            P(("groups", "out"), None, None),
            P(("groups", "out"), None, None),
            P(("groups", "out"), None, None),
        ),
        out_specs=P("groups", "out"),
        check_vma=False,
    )
```

```python
import math

import jax
import jax.numpy as jnp
from jax import lax
from jax.experimental import pallas as pl
from jax.experimental.pallas import tpu as pltpu
from jax.sharding import PartitionSpec as P

HQ = 48
KVH = 4
HD = 128


rope_base = 1000000.0
norm_eps = 1e-05


def rotate(vec, position):
    half = vec.shape[-1] // 2
    index = jnp.arange(half, dtype=jnp.float32)
    freq = jnp.exp(index * (-2.0 * math.log(rope_base) / vec.shape[-1]))
    angle = position * freq
    cosine = jnp.cos(angle)
    sine = jnp.sin(angle)
    first = vec[..., :half]
    second = vec[..., half:]
    return jnp.concatenate(
        [first * cosine - second * sine, second * cosine + first * sine], axis=-1
    )


def dequant(cache, scales):
    rows, span, width = cache.shape
    blocks = scales.shape[1]
    factor = jnp.exp2(scales.astype(jnp.float32)).astype(jnp.bfloat16)
    shaped = cache.reshape(rows, blocks, span // blocks, KVH, width // KVH)
    return (shaped * factor[:, :, None, :, None]).reshape(rows, span, KVH, width // KVH)


def per_device_general(
    stream,
    norm_gain,
    w_query,
    w_keyval,
    w_out,
    lengths,
    key_cache,
    value_cache,
    key_scales,
    value_scales,
):
    local_rows = lengths.shape[0]
    xf = stream.astype(jnp.float32)
    whole = lax.all_gather(stream, "out", axis=1, tiled=True).astype(jnp.float32)
    meansq = jnp.mean(whole * whole, axis=-1, keepdims=True)
    normed = (whole * lax.rsqrt(meansq + norm_eps) * norm_gain).astype(jnp.bfloat16)
    q_local = jnp.dot(normed, w_query, preferred_element_type=jnp.float32).astype(jnp.bfloat16)
    kv_local = jnp.dot(normed, w_keyval, preferred_element_type=jnp.float32).astype(jnp.bfloat16)
    q_rows, kv_rows = (
        lax.all_to_all(q_local, "out", split_axis=0, concat_axis=1, tiled=True),
        lax.all_to_all(kv_local, "out", split_axis=0, concat_axis=1, tiled=True),
    )
    position = lengths.astype(jnp.float32)[:, None, None]
    rotated = rotate(q_rows.astype(jnp.float32).reshape(local_rows, HQ, HD), position).astype(
        jnp.bfloat16
    )
    rotated = rotated.reshape(local_rows, KVH, HQ // KVH, HD)
    new_key = rotate(
        kv_rows[:, : KVH * HD].astype(jnp.float32).reshape(local_rows, KVH, HD), position
    ).astype(jnp.bfloat16)
    new_value = kv_rows[:, KVH * HD :].reshape(local_rows, KVH, HD)
    factor = HD ** (-0.5)
    own = jnp.einsum("rkgd,rkd->rkg", rotated, new_key, preferred_element_type=jnp.float32) * factor
    span = key_cache.shape[1]
    scores = (
        jnp.einsum(
            "rkgd,rjkd->rkgj",
            rotated,
            dequant(key_cache, key_scales),
            preferred_element_type=jnp.float32,
        )
        * factor
    )
    valid = jnp.arange(span, dtype=jnp.int32)[None, :] < lengths[:, None]
    scores = jnp.where(valid[:, None, None, :], scores, -jnp.inf)
    top = jnp.maximum(jnp.max(scores, axis=-1), own)
    weights = jnp.exp(scores - top[..., None])
    own_weight = jnp.exp(own - top)
    total = jnp.sum(weights, axis=-1) + own_weight
    own_rounded = lax.optimization_barrier(own_weight.astype(jnp.bfloat16)).astype(jnp.float32)
    summed = jnp.einsum(
        "rkgj,rjkd->rkgd",
        weights.astype(jnp.bfloat16),
        dequant(value_cache, value_scales),
        preferred_element_type=jnp.float32,
    )
    summed = summed + own_rounded[..., None] * new_value.astype(jnp.float32)[:, :, None, :]
    attended = (summed / total[..., None]).astype(jnp.bfloat16).reshape(local_rows, HQ * HD)
    heads = lax.all_to_all(attended, "out", split_axis=1, concat_axis=0, tiled=True)
    partial_terms = jnp.dot(heads, w_out, preferred_element_type=jnp.float32)
    projected = lax.psum_scatter(partial_terms, "out", scatter_dimension=1, tiled=True)
    return (xf + projected).astype(jnp.bfloat16)


def swapped(value, bit, size):
    return lax.ppermute(value, "out", [(i, i ^ bit) for i in range(size)])


def project_kernel(order, pieces, me_ref, *refs):
    shards = refs[:pieces]
    gain_ref, wq_ref, wkv_ref, out_ref = refs[pieces:]
    rows, depth = shards[0].shape
    columns, kv_columns = wq_ref.shape[1], wkv_ref.shape[0]
    targets, per_target, _ = out_ref.shape
    me = me_ref[0]
    square = jnp.zeros((rows, 128), jnp.float32)
    for k in range(pieces):
        part = shards[k][...].astype(jnp.float32)
        part = part * part
        for lane in range(0, depth, 128):
            square += part[:, lane : lane + 128]
    meansq = jnp.sum(square, axis=-1, keepdims=True) / (depth * pieces)
    inverse = lax.rsqrt(meansq + norm_eps)
    q_sum = jnp.zeros((rows, columns), jnp.float32)
    kv_sum = jnp.zeros((rows, kv_columns), jnp.float32)
    for k in range(pieces):
        start = pl.multiple_of(lax.bitwise_xor(me, order[k]) * depth, 128)
        gain = gain_ref[:, pl.ds(start, depth)]
        normed = (shards[k][...].astype(jnp.float32) * inverse * gain).astype(jnp.bfloat16)
        kv_sum += lax.dot_general(
            normed,
            wkv_ref[:, pl.ds(start, depth)],
            (((1,), (1,)), ((), ())),
            preferred_element_type=jnp.float32,
        )
        q_sum += jnp.dot(normed, wq_ref[pl.ds(start, depth), :], preferred_element_type=jnp.float32)
    odd = lax.bitwise_and(me, 1).astype(jnp.float32)
    both = jnp.concatenate([kv_sum * (1.0 - odd), kv_sum * odd], axis=-1)
    for k in range(targets):
        take = slice(k * per_target, (k + 1) * per_target)
        out_ref[k, :, :columns] = q_sum[take].astype(jnp.bfloat16)
        out_ref[k, :, columns:] = both[take].astype(jnp.bfloat16)


def project(me, order, shards, norm_gain, w_query, w_keyval, per_target):
    pieces = len(shards)
    rows = shards[0].shape[0]
    vmem = pl.BlockSpec(memory_space=pltpu.VMEM)
    return pl.pallas_call(
        lambda *refs: project_kernel(order, pieces, *refs),
        out_shape=jax.ShapeDtypeStruct(
            (rows // per_target, per_target, w_query.shape[1] + 2 * w_keyval.shape[1]), jnp.bfloat16
        ),
        in_specs=[pl.BlockSpec(memory_space=pltpu.SMEM)] + [vmem] * (pieces + 3),
        out_specs=vmem,
        compiler_params=pltpu.CompilerParams(vmem_limit_bytes=16 * 1024 * 1024),
        name="project",
    )(me, *shards, norm_gain.reshape(1, -1), w_query, w_keyval.T)


def attend_kernel(
    lengths_ref, rows_ref, cos_ref, sin_ref, kf_ref, vf_ref, keys_ref, values_ref, out_ref
):
    sources, local_rows, _ = rows_ref.shape
    span = keys_ref.shape[1]
    each = out_ref.shape[-1] // HD
    heads = each * sources
    per_key = HQ // KVH // each
    per_block = span // kf_ref.shape[-1]
    source = lax.broadcasted_iota(jnp.int32, (heads, HD), 0) % sources
    key_head = source // per_key
    pick_row = lax.broadcasted_iota(jnp.int32, (2 * sources, sources), 0)
    pick_col = lax.broadcasted_iota(jnp.int32, (2 * sources, sources), 1)
    wanted = (pick_row % sources) // per_key + KVH * (pick_row // sources)
    pick = (pick_col // 2 == wanted).astype(jnp.bfloat16)
    place = lax.broadcasted_iota(jnp.int32, (heads, span), 1)
    for r in range(local_rows):
        got = rows_ref[:, r, :].astype(jnp.float32)
        cosine = cos_ref[r : r + 1, :]
        sine = sin_ref[r : r + 1, :]

        def turn(vec):
            return (vec * cosine + pltpu.roll(vec, HD // 2, 1) * sine).astype(jnp.bfloat16)

        query = turn(
            jnp.concatenate([got[:, g * HD : (g + 1) * HD] for g in range(each)], axis=0)
        )
        fresh = jnp.dot(
            pick, got[:, each * HD :].astype(jnp.bfloat16), preferred_element_type=jnp.float32
        )
        new_key = turn(fresh[:sources]).astype(jnp.float32)
        new_key = jnp.concatenate([new_key] * each, axis=0)
        new_value = jnp.concatenate([fresh[sources:]] * each, axis=0)
        wide = jnp.concatenate(
            [jnp.where(key_head == k, query, jnp.zeros_like(query)) for k in range(KVH)], axis=1
        )
        scores = lax.dot_general(
            wide, keys_ref[r], (((1,), (1,)), ((), ())), preferred_element_type=jnp.float32
        )
        kf = kf_ref[r]
        vf = vf_ref[r]
        scores = jnp.concatenate(
            [
                scores[:, b * per_block : (b + 1) * per_block] * kf[:, b : b + 1]
                for b in range(kf.shape[1])
            ],
            axis=1,
        )
        scores = jnp.where(place < lengths_ref[r], scores * HD ** (-0.5), -jnp.inf)
        own = jnp.sum(query.astype(jnp.float32) * new_key, axis=-1, keepdims=True) * HD ** (-0.5)
        top = jnp.maximum(jnp.max(scores, axis=-1, keepdims=True), own)
        weights = jnp.exp(scores - top)
        own_weight = jnp.exp(own - top)
        total = jnp.sum(weights, axis=-1, keepdims=True) + own_weight
        rounded = weights.astype(jnp.bfloat16).astype(jnp.float32)
        rounded = jnp.concatenate(
            [
                rounded[:, b * per_block : (b + 1) * per_block] * vf[:, b : b + 1]
                for b in range(vf.shape[1])
            ],
            axis=1,
        ).astype(jnp.bfloat16)
        summed = jnp.dot(rounded, values_ref[r], preferred_element_type=jnp.float32)
        mine = summed[:, :HD]
        for k in range(1, KVH):
            mine = jnp.where(key_head == k, summed[:, k * HD : (k + 1) * HD], mine)
        mine = mine + own_weight.astype(jnp.bfloat16).astype(jnp.float32) * new_value
        mine = (mine / total).astype(jnp.bfloat16)
        for g in range(each):
            out_ref[:, r, g * HD : (g + 1) * HD] = mine[g * sources : (g + 1) * sources]


def attend(rows, columns, lengths, key_cache, value_cache, key_scales, value_scales):
    sources, local_rows, _ = rows.shape
    half = HD // 2
    freq = jnp.exp(jnp.arange(half, dtype=jnp.float32) * (-2.0 * math.log(rope_base) / HD))
    angle = lengths.astype(jnp.float32)[:, None] * freq
    cosine, sine = jnp.cos(angle), jnp.sin(angle)
    each = columns // HD
    key_head = jnp.tile(jnp.arange(sources) // (HQ // KVH // each), each)

    def spread(scales):
        return jnp.swapaxes(jnp.exp2(scales.astype(jnp.float32))[:, :, key_head], 1, 2)

    vmem = pl.BlockSpec(memory_space=pltpu.VMEM)
    return pl.pallas_call(
        attend_kernel,
        out_shape=jax.ShapeDtypeStruct((sources, local_rows, columns), jnp.bfloat16),
        in_specs=[pl.BlockSpec(memory_space=pltpu.SMEM)] + [vmem] * 7,
        out_specs=vmem,
        compiler_params=pltpu.CompilerParams(vmem_limit_bytes=8 * 1024 * 1024),
        name="attend",
    )(
        lengths,
        rows,
        jnp.concatenate([cosine, cosine], axis=-1),
        jnp.concatenate([-sine, sine], axis=-1),
        spread(key_scales),
        spread(value_scales),
        key_cache,
        value_cache,
    )


def expand_kernel(order, me_ref, heads_ref, w_ref, out_ref):
    width = out_ref.shape[-1]
    me = me_ref[0]
    heads = jnp.concatenate(
        [heads_ref[k].astype(jnp.float32) for k in range(heads_ref.shape[0])], axis=0
    ).astype(jnp.bfloat16)
    for k in range(len(order)):
        start = pl.multiple_of(lax.bitwise_xor(me, order[k]) * width, 128)
        out_ref[k] = jnp.dot(
            heads, w_ref[:, pl.ds(start, width)], preferred_element_type=jnp.float32
        ).astype(out_ref.dtype)


def expand(me, order, heads, w_out, width, dtype):
    vmem = pl.BlockSpec(memory_space=pltpu.VMEM)
    return pl.pallas_call(
        lambda *refs: expand_kernel(order, *refs),
        out_shape=jax.ShapeDtypeStruct(
            (len(order), heads.shape[0] * heads.shape[1], width), dtype
        ),
        in_specs=[pl.BlockSpec(memory_space=pltpu.SMEM), vmem, vmem],
        out_specs=vmem,
        compiler_params=pltpu.CompilerParams(vmem_limit_bytes=16 * 1024 * 1024),
        name="expand",
    )(me, heads, w_out)


def per_device(
    size,
    stream,
    norm_gain,
    w_query,
    w_keyval,
    w_out,
    lengths,
    key_cache,
    value_cache,
    key_scales,
    value_scales,
):
    local_rows = lengths.shape[0]
    me = lax.axis_index("out").astype(jnp.int32)[None]
    width = stream.shape[1]
    columns = w_query.shape[1]

    bits = [1 << k for k in reversed(range(size.bit_length() - 1))]
    held = {0: stream}
    for bit in bits:
        for mask in list(held):
            held[mask | bit] = swapped(held[mask], bit, size)
    order = list(held)
    qkv = project(me, order, [held[m] for m in order], norm_gain, w_query, w_keyval, local_rows)
    rows = lax.all_to_all(qkv, "out", split_axis=0, concat_axis=0, tiled=True)
    attended = attend(rows, columns, lengths, key_cache, value_cache, key_scales, value_scales)
    heads = lax.all_to_all(attended, "out", split_axis=0, concat_axis=0, tiled=True)

    away = [m for m in range(size - 1, -1, -1) if m & 1]
    near = [m ^ 1 for m in away]
    sent = swapped(expand(me, away, heads, w_out, width, jnp.bfloat16), 1, size)
    kept = expand(me, near, heads, w_out, width, jnp.float32)
    owed = {m: kept[k] + sent[k].astype(jnp.float32) for k, m in enumerate(near)}
    for bit in bits[-2::-1]:
        for mask in sorted((m for m in owed if m & bit), reverse=True):
            got = swapped(owed.pop(mask).astype(jnp.bfloat16), bit, size)
            owed[mask ^ bit] = owed[mask ^ bit] + got.astype(jnp.float32)
    return (stream.astype(jnp.float32) + owed[0]).astype(jnp.bfloat16)


def solution(mesh):
    size = mesh.shape["out"]

    def step(stream, *rest):
        columns = rest[1].shape[1]
        whole_heads = columns % HD == 0 and HQ // KVH * HD % columns == 0 and 2 * rest[2].shape[1] == HD
        if size & (size - 1) == 0 and stream.shape[1] % 128 == 0 and whole_heads:
            return per_device(size, stream, *rest)
        return per_device_general(stream, *rest)

    return jax.shard_map(
        step,
        mesh=mesh,
        in_specs=(
            P("groups", "out"),
            P(),
            P(None, "out"),
            P(None, "out"),
            P("out", None),
            P(("groups", "out")),
            P(("groups", "out"), None, None),
            P(("groups", "out"), None, None),
            P(("groups", "out"), None, None),
            P(("groups", "out"), None, None),
        ),
        out_specs=P("groups", "out"),
        check_vma=False,
    )
```

```python
import math

import jax
import jax.numpy as jnp
from jax import lax
from jax.experimental import pallas as pl
from jax.experimental.pallas import tpu as pltpu
from jax.sharding import PartitionSpec as P

HQ = 48
KVH = 4
HD = 128


rope_base = 1000000.0
norm_eps = 1e-05


def rotate(vec, position):
    half = vec.shape[-1] // 2
    index = jnp.arange(half, dtype=jnp.float32)
    freq = jnp.exp(index * (-2.0 * math.log(rope_base) / vec.shape[-1]))
    angle = position * freq
    cosine = jnp.cos(angle)
    sine = jnp.sin(angle)
    first = vec[..., :half]
    second = vec[..., half:]
    return jnp.concatenate(
        [first * cosine - second * sine, second * cosine + first * sine], axis=-1
    )


def dequant(cache, scales):
    rows, span, width = cache.shape
    blocks = scales.shape[1]
    factor = jnp.exp2(scales.astype(jnp.float32)).astype(jnp.bfloat16)
    shaped = cache.reshape(rows, blocks, span // blocks, KVH, width // KVH)
    return (shaped * factor[:, :, None, :, None]).reshape(rows, span, KVH, width // KVH)


def per_device_general(
    stream,
    norm_gain,
    w_query,
    w_keyval,
    w_out,
    lengths,
    key_cache,
    value_cache,
    key_scales,
    value_scales,
):
    local_rows = lengths.shape[0]
    xf = stream.astype(jnp.float32)
    whole = lax.all_gather(stream, "out", axis=1, tiled=True).astype(jnp.float32)
    meansq = jnp.mean(whole * whole, axis=-1, keepdims=True)
    normed = (whole * lax.rsqrt(meansq + norm_eps) * norm_gain).astype(jnp.bfloat16)
    q_local = jnp.dot(normed, w_query, preferred_element_type=jnp.float32).astype(jnp.bfloat16)
    kv_local = jnp.dot(normed, w_keyval, preferred_element_type=jnp.float32).astype(jnp.bfloat16)
    q_rows, kv_rows = (
        lax.all_to_all(q_local, "out", split_axis=0, concat_axis=1, tiled=True),
        lax.all_to_all(kv_local, "out", split_axis=0, concat_axis=1, tiled=True),
    )
    position = lengths.astype(jnp.float32)[:, None, None]
    rotated = rotate(q_rows.astype(jnp.float32).reshape(local_rows, HQ, HD), position).astype(
        jnp.bfloat16
    )
    rotated = rotated.reshape(local_rows, KVH, HQ // KVH, HD)
    new_key = rotate(
        kv_rows[:, : KVH * HD].astype(jnp.float32).reshape(local_rows, KVH, HD), position
    ).astype(jnp.bfloat16)
    new_value = kv_rows[:, KVH * HD :].reshape(local_rows, KVH, HD)
    factor = HD ** (-0.5)
    own = jnp.einsum("rkgd,rkd->rkg", rotated, new_key, preferred_element_type=jnp.float32) * factor
    span = key_cache.shape[1]
    scores = (
        jnp.einsum(
            "rkgd,rjkd->rkgj",
            rotated,
            dequant(key_cache, key_scales),
            preferred_element_type=jnp.float32,
        )
        * factor
    )
    valid = jnp.arange(span, dtype=jnp.int32)[None, :] < lengths[:, None]
    scores = jnp.where(valid[:, None, None, :], scores, -jnp.inf)
    top = jnp.maximum(jnp.max(scores, axis=-1), own)
    weights = jnp.exp(scores - top[..., None])
    own_weight = jnp.exp(own - top)
    total = jnp.sum(weights, axis=-1) + own_weight
    own_rounded = lax.optimization_barrier(own_weight.astype(jnp.bfloat16)).astype(jnp.float32)
    summed = jnp.einsum(
        "rkgj,rjkd->rkgd",
        weights.astype(jnp.bfloat16),
        dequant(value_cache, value_scales),
        preferred_element_type=jnp.float32,
    )
    summed = summed + own_rounded[..., None] * new_value.astype(jnp.float32)[:, :, None, :]
    attended = (summed / total[..., None]).astype(jnp.bfloat16).reshape(local_rows, HQ * HD)
    heads = lax.all_to_all(attended, "out", split_axis=1, concat_axis=0, tiled=True)
    partial_terms = jnp.dot(heads, w_out, preferred_element_type=jnp.float32)
    projected = lax.psum_scatter(partial_terms, "out", scatter_dimension=1, tiled=True)
    return (xf + projected).astype(jnp.bfloat16)


def swapped(value, bit, size):
    return lax.ppermute(value, "out", [(i, i ^ bit) for i in range(size)])


def stage_kernel(in_ref, *refs):
    refs[-1][...] = in_ref[...]


def stage(value, *beside):
    vmem = pl.BlockSpec(memory_space=pltpu.VMEM)
    return pl.pallas_call(
        stage_kernel,
        out_shape=jax.ShapeDtypeStruct(value.shape, value.dtype),
        in_specs=[vmem] + [pl.BlockSpec(memory_space=pl.ANY)] * len(beside),
        out_specs=vmem,
        compiler_params=pltpu.CompilerParams(vmem_limit_bytes=2 * 1024 * 1024),
        name="stage",
    )(value, *beside)


def project_kernel(order, pieces, *refs):
    shards = refs[:pieces]
    gain_ref, wq_ref, wkv_ref, out_ref = refs[pieces:]
    rows, depth = shards[0].shape
    columns, kv_columns = wq_ref.shape[1], wkv_ref.shape[0]
    targets, per_target, _ = out_ref.shape
    me = lax.axis_index("out")
    square = jnp.zeros((rows, 128), jnp.float32)
    for k in range(pieces):
        part = shards[k][...].astype(jnp.float32)
        part = part * part
        for lane in range(0, depth, 128):
            square += part[:, lane : lane + 128]
    meansq = jnp.sum(square, axis=-1, keepdims=True) / (depth * pieces)
    inverse = lax.rsqrt(meansq + norm_eps)
    q_sum = jnp.zeros((rows, columns), jnp.float32)
    kv_sum = jnp.zeros((rows, kv_columns), jnp.float32)
    for k in range(pieces):
        start = pl.multiple_of(lax.bitwise_xor(me, order[k]) * depth, 128)
        gain = gain_ref[:, pl.ds(start, depth)]
        normed = (shards[k][...].astype(jnp.float32) * inverse * gain).astype(jnp.bfloat16)
        kv_sum += lax.dot_general(
            normed,
            wkv_ref[:, pl.ds(start, depth)],
            (((1,), (1,)), ((), ())),
            preferred_element_type=jnp.float32,
        )
        q_sum += jnp.dot(normed, wq_ref[pl.ds(start, depth), :], preferred_element_type=jnp.float32)
    odd = lax.bitwise_and(me, 1).astype(jnp.float32)
    both = jnp.concatenate([kv_sum * (1.0 - odd), kv_sum * odd], axis=-1)
    for k in range(targets):
        take = slice(k * per_target, (k + 1) * per_target)
        out_ref[k, :, :columns] = q_sum[take].astype(jnp.bfloat16)
        out_ref[k, :, columns:] = both[take].astype(jnp.bfloat16)


def project(order, shards, norm_gain, w_query, w_keyval, per_target):
    pieces = len(shards)
    rows = shards[0].shape[0]
    vmem = pl.BlockSpec(memory_space=pltpu.VMEM)
    return pl.pallas_call(
        lambda *refs: project_kernel(order, pieces, *refs),
        out_shape=jax.ShapeDtypeStruct(
            (rows // per_target, per_target, w_query.shape[1] + 2 * w_keyval.shape[0]), jnp.bfloat16
        ),
        in_specs=[vmem] * (pieces + 3),
        out_specs=vmem,
        compiler_params=pltpu.CompilerParams(vmem_limit_bytes=16 * 1024 * 1024),
        name="project",
    )(*shards, norm_gain, w_query, w_keyval)


def attend_kernel(
    lengths_ref, rows_ref, cos_ref, sin_ref, kf_ref, vf_ref, keys_ref, values_ref, out_ref
):
    sources, local_rows, _ = rows_ref.shape
    span = keys_ref.shape[1]
    each = out_ref.shape[-1] // HD
    heads = each * sources
    per_key = HQ // KVH // each
    blocks = kf_ref.shape[1]
    per_block = span // blocks
    source = lax.broadcasted_iota(jnp.int32, (heads, HD), 0) % sources
    key_head = source // per_key
    pick_row = lax.broadcasted_iota(jnp.int32, (2 * sources, sources), 0)
    pick_col = lax.broadcasted_iota(jnp.int32, (2 * sources, sources), 1)
    wanted = (pick_row % sources) // per_key + KVH * (pick_row // sources)
    pick = (pick_col // 2 == wanted).astype(jnp.bfloat16)
    place = lax.broadcasted_iota(jnp.int32, (heads, span), 1)
    block_head = lax.broadcasted_iota(jnp.int32, (heads, per_block), 0) % sources // per_key

    def scaled(values, scale_ref, r):
        parts = []
        for b in range(blocks):
            scale = jnp.full((heads, per_block), scale_ref[r, b, 0])
            for k in range(1, KVH):
                scale = jnp.where(block_head == k, scale_ref[r, b, k], scale)
            parts.append(values[:, b * per_block : (b + 1) * per_block] * scale)
        return jnp.concatenate(parts, axis=1)

    for r in range(local_rows):
        got = rows_ref[:, r, :].astype(jnp.float32)
        cosine = cos_ref[r : r + 1, :]
        sine = sin_ref[r : r + 1, :]

        def turn(vec):
            return (vec * cosine + pltpu.roll(vec, HD // 2, 1) * sine).astype(jnp.bfloat16)

        query = turn(
            jnp.concatenate([got[:, g * HD : (g + 1) * HD] for g in range(each)], axis=0)
        )
        fresh = jnp.dot(
            pick, got[:, each * HD :].astype(jnp.bfloat16), preferred_element_type=jnp.float32
        )
        new_key = turn(fresh[:sources]).astype(jnp.float32)
        new_key = jnp.concatenate([new_key] * each, axis=0)
        new_value = jnp.concatenate([fresh[sources:]] * each, axis=0)
        wide = jnp.concatenate(
            [jnp.where(key_head == k, query, jnp.zeros_like(query)) for k in range(KVH)], axis=1
        )
        scores = lax.dot_general(
            wide, keys_ref[r], (((1,), (1,)), ((), ())), preferred_element_type=jnp.float32
        )
        scores = scaled(scores, kf_ref, r)
        scores = jnp.where(place < lengths_ref[r], scores * HD ** (-0.5), -jnp.inf)
        own = jnp.sum(query.astype(jnp.float32) * new_key, axis=-1, keepdims=True) * HD ** (-0.5)
        top = jnp.maximum(jnp.max(scores, axis=-1, keepdims=True), own)
        weights = jnp.exp(scores - top)
        own_weight = jnp.exp(own - top)
        total = jnp.sum(weights, axis=-1, keepdims=True) + own_weight
        rounded = weights.astype(jnp.bfloat16).astype(jnp.float32)
        rounded = scaled(rounded, vf_ref, r).astype(jnp.bfloat16)
        summed = jnp.dot(rounded, values_ref[r], preferred_element_type=jnp.float32)
        mine = summed[:, :HD]
        for k in range(1, KVH):
            mine = jnp.where(key_head == k, summed[:, k * HD : (k + 1) * HD], mine)
        mine = mine + own_weight.astype(jnp.bfloat16).astype(jnp.float32) * new_value
        mine = (mine / total).astype(jnp.bfloat16)
        for g in range(each):
            out_ref[:, r, g * HD : (g + 1) * HD] = mine[g * sources : (g + 1) * sources]


def attend(rows, columns, lengths, cosine, sine, key_factors, value_factors, key_cache, value_cache):
    sources, local_rows, _ = rows.shape
    smem = pl.BlockSpec(memory_space=pltpu.SMEM)
    vmem = pl.BlockSpec(memory_space=pltpu.VMEM)
    return pl.pallas_call(
        attend_kernel,
        out_shape=jax.ShapeDtypeStruct((sources, local_rows, columns), jnp.bfloat16),
        in_specs=[smem] + [vmem] * 3 + [smem] * 2 + [vmem] * 2,
        out_specs=vmem,
        compiler_params=pltpu.CompilerParams(vmem_limit_bytes=8 * 1024 * 1024),
        name="attend",
    )(lengths, rows, cosine, sine, key_factors, value_factors, key_cache, value_cache)


def expand_kernel(order, heads_ref, w_ref, out_ref):
    width = out_ref.shape[-1]
    me = lax.axis_index("out")
    heads = jnp.concatenate(
        [heads_ref[k].astype(jnp.float32) for k in range(heads_ref.shape[0])], axis=0
    ).astype(jnp.bfloat16)
    for k in range(len(order)):
        start = pl.multiple_of(lax.bitwise_xor(me, order[k]) * width, 128)
        out_ref[k] = jnp.dot(
            heads, w_ref[:, pl.ds(start, width)], preferred_element_type=jnp.float32
        ).astype(out_ref.dtype)


def expand(order, heads, w_out, width, dtype):
    vmem = pl.BlockSpec(memory_space=pltpu.VMEM)
    return pl.pallas_call(
        lambda *refs: expand_kernel(order, *refs),
        out_shape=jax.ShapeDtypeStruct(
            (len(order), heads.shape[0] * heads.shape[1], width), dtype
        ),
        in_specs=[vmem, vmem],
        out_specs=vmem,
        compiler_params=pltpu.CompilerParams(vmem_limit_bytes=16 * 1024 * 1024),
        name="expand",
    )(heads, w_out)


def per_device(
    size,
    stream,
    norm_gain,
    w_query,
    w_keyval,
    w_out,
    lengths,
    key_cache,
    value_cache,
    key_scales,
    value_scales,
):
    local_rows = lengths.shape[0]
    width = stream.shape[1]
    columns = w_query.shape[1]

    bits = [1 << k for k in reversed(range(size.bit_length() - 1))]
    held = {0: stream}
    w_keyval = w_keyval.T
    norm_gain = norm_gain.reshape(1, -1)
    for bit in bits:
        for mask in list(held):
            held[mask | bit] = swapped(stream if mask == 0 else held[mask], bit, size)
        if bit == bits[0]:
            held[0] = stage(stream, *[w_keyval] * (5 * w_query.size // w_keyval.size))
            held[0], held[bit] = lax.optimization_barrier((held[0], held[bit]))
        if bit == bits[1]:
            norm_gain = stage(norm_gain)
            norm_gain, held[bit] = lax.optimization_barrier((norm_gain, held[bit]))
    order = list(held)
    freq = jnp.exp(
        jnp.arange(HD // 2, dtype=jnp.float32) * (-2.0 * math.log(rope_base) / HD)
    )
    angle = lengths.astype(jnp.float32)[:, None] * freq
    cosine, sine = jnp.cos(angle), jnp.sin(angle)
    side = (
        jnp.concatenate([cosine, cosine], axis=-1),
        jnp.concatenate([-sine, sine], axis=-1),
        jnp.exp2(key_scales.astype(jnp.float32)),
        jnp.exp2(value_scales.astype(jnp.float32)),
    )
    side, held[size - 1] = lax.optimization_barrier((side, held[size - 1]))
    qkv = project(order, [held[m] for m in order], norm_gain, w_query, w_keyval, local_rows)
    rows = lax.all_to_all(qkv, "out", split_axis=0, concat_axis=0, tiled=True)
    attended = attend(rows, columns, lengths, *side, key_cache, value_cache)
    heads = lax.all_to_all(attended, "out", split_axis=0, concat_axis=0, tiled=True)

    away = [m for m in range(size - 1, -1, -1) if m & 1]
    near = [m ^ 1 for m in away]
    sent = swapped(expand(away, heads, w_out, width, jnp.bfloat16), 1, size)
    kept = expand(near, heads, w_out, width, jnp.float32)
    owed = {m: kept[k] + sent[k].astype(jnp.float32) for k, m in enumerate(near)}
    for bit in bits[-2::-1]:
        for mask in sorted((m for m in owed if m & bit), reverse=True):
            got = swapped(owed.pop(mask).astype(jnp.bfloat16), bit, size)
            owed[mask ^ bit] = owed[mask ^ bit] + got.astype(jnp.float32)
    return (stream.astype(jnp.float32) + owed[0]).astype(jnp.bfloat16)


def solution(mesh):
    size = mesh.shape["out"]

    def step(stream, *rest):
        columns = rest[1].shape[1]
        whole_heads = columns % HD == 0 and HQ // KVH * HD % columns == 0 and 2 * rest[2].shape[1] == HD
        if size & (size - 1) == 0 and stream.shape[1] % 128 == 0 and whole_heads:
            return per_device(size, stream, *rest)
        return per_device_general(stream, *rest)

    return jax.shard_map(
        step,
        mesh=mesh,
        in_specs=(
            P("groups", "out"),
            P(),
            P(None, "out"),
            P(None, "out"),
            P("out", None),
            P(("groups", "out")),
            P(("groups", "out"), None, None),
            P(("groups", "out"), None, None),
            P(("groups", "out"), None, None),
            P(("groups", "out"), None, None),
        ),
        out_specs=P("groups", "out"),
        check_vma=False,
    )
```

```python
import math

import jax
import jax.numpy as jnp
from jax import lax
from jax.experimental import pallas as pl
from jax.experimental.pallas import tpu as pltpu
from jax.sharding import PartitionSpec as P

HQ = 48
KVH = 4
HD = 128


rope_base = 1000000.0
norm_eps = 1e-05


def rotate(vec, position):
    half = vec.shape[-1] // 2
    index = jnp.arange(half, dtype=jnp.float32)
    freq = jnp.exp(index * (-2.0 * math.log(rope_base) / vec.shape[-1]))
    angle = position * freq
    cosine = jnp.cos(angle)
    sine = jnp.sin(angle)
    first = vec[..., :half]
    second = vec[..., half:]
    return jnp.concatenate(
        [first * cosine - second * sine, second * cosine + first * sine], axis=-1
    )


def dequant(cache, scales):
    rows, span, width = cache.shape
    blocks = scales.shape[1]
    factor = jnp.exp2(scales.astype(jnp.float32)).astype(jnp.bfloat16)
    shaped = cache.reshape(rows, blocks, span // blocks, KVH, width // KVH)
    return (shaped * factor[:, :, None, :, None]).reshape(rows, span, KVH, width // KVH)


def per_device_general(
    stream,
    norm_gain,
    w_query,
    w_keyval,
    w_out,
    lengths,
    key_cache,
    value_cache,
    key_scales,
    value_scales,
):
    local_rows = lengths.shape[0]
    xf = stream.astype(jnp.float32)
    whole = lax.all_gather(stream, "out", axis=1, tiled=True).astype(jnp.float32)
    meansq = jnp.mean(whole * whole, axis=-1, keepdims=True)
    normed = (whole * lax.rsqrt(meansq + norm_eps) * norm_gain).astype(jnp.bfloat16)
    q_local = jnp.dot(normed, w_query, preferred_element_type=jnp.float32).astype(jnp.bfloat16)
    kv_local = jnp.dot(normed, w_keyval, preferred_element_type=jnp.float32).astype(jnp.bfloat16)
    q_rows, kv_rows = (
        lax.all_to_all(q_local, "out", split_axis=0, concat_axis=1, tiled=True),
        lax.all_to_all(kv_local, "out", split_axis=0, concat_axis=1, tiled=True),
    )
    position = lengths.astype(jnp.float32)[:, None, None]
    rotated = rotate(q_rows.astype(jnp.float32).reshape(local_rows, HQ, HD), position).astype(
        jnp.bfloat16
    )
    rotated = rotated.reshape(local_rows, KVH, HQ // KVH, HD)
    new_key = rotate(
        kv_rows[:, : KVH * HD].astype(jnp.float32).reshape(local_rows, KVH, HD), position
    ).astype(jnp.bfloat16)
    new_value = kv_rows[:, KVH * HD :].reshape(local_rows, KVH, HD)
    factor = HD ** (-0.5)
    own = jnp.einsum("rkgd,rkd->rkg", rotated, new_key, preferred_element_type=jnp.float32) * factor
    span = key_cache.shape[1]
    scores = (
        jnp.einsum(
            "rkgd,rjkd->rkgj",
            rotated,
            dequant(key_cache, key_scales),
            preferred_element_type=jnp.float32,
        )
        * factor
    )
    valid = jnp.arange(span, dtype=jnp.int32)[None, :] < lengths[:, None]
    scores = jnp.where(valid[:, None, None, :], scores, -jnp.inf)
    top = jnp.maximum(jnp.max(scores, axis=-1), own)
    weights = jnp.exp(scores - top[..., None])
    own_weight = jnp.exp(own - top)
    total = jnp.sum(weights, axis=-1) + own_weight
    own_rounded = lax.optimization_barrier(own_weight.astype(jnp.bfloat16)).astype(jnp.float32)
    summed = jnp.einsum(
        "rkgj,rjkd->rkgd",
        weights.astype(jnp.bfloat16),
        dequant(value_cache, value_scales),
        preferred_element_type=jnp.float32,
    )
    summed = summed + own_rounded[..., None] * new_value.astype(jnp.float32)[:, :, None, :]
    attended = (summed / total[..., None]).astype(jnp.bfloat16).reshape(local_rows, HQ * HD)
    heads = lax.all_to_all(attended, "out", split_axis=1, concat_axis=0, tiled=True)
    partial_terms = jnp.dot(heads, w_out, preferred_element_type=jnp.float32)
    projected = lax.psum_scatter(partial_terms, "out", scatter_dimension=1, tiled=True)
    return (xf + projected).astype(jnp.bfloat16)


def swapped(value, mask, size, label):
    with jax.named_scope(label):
        return lax.ppermute(value, "out", [(i, i ^ mask) for i in range(size)])


def room_kernel(out_ref):
    pass


def stage_kernel(*refs):
    refs[-1][...] = jnp.zeros_like(refs[-1])


def stage(cover):
    vmem = pl.BlockSpec(memory_space=pltpu.VMEM)
    small = pltpu.CompilerParams(vmem_limit_bytes=2 * 1024 * 1024)
    room = pl.pallas_call(
        room_kernel,
        out_shape=jax.ShapeDtypeStruct((2048, 512), jnp.bfloat16),
        out_specs=vmem,
        compiler_params=small,
        name="room",
    )()
    count = -(-cover // (2 * room.size))
    return pl.pallas_call(
        stage_kernel,
        out_shape=jax.ShapeDtypeStruct((8, 128), jnp.float32),
        in_specs=[pl.BlockSpec(memory_space=pl.ANY)] * count,
        out_specs=vmem,
        compiler_params=small,
        name="stage",
    )(*[room] * count)


def project_kernel(order, pieces, *refs):
    shards = refs[:pieces]
    gain_ref, wq_ref, wkv_ref, _, out_ref = refs[pieces:]
    rows, depth = shards[0].shape
    columns, kv_columns = wq_ref.shape[1], wkv_ref.shape[0]
    targets, per_target, _ = out_ref.shape
    me = lax.axis_index("out")
    square = jnp.zeros((rows, 128), jnp.float32)
    for k in range(pieces):
        part = shards[k][...].astype(jnp.float32)
        part = part * part
        for lane in range(0, depth, 128):
            square += part[:, lane : lane + 128]
    meansq = jnp.sum(square, axis=-1, keepdims=True) / (depth * pieces)
    inverse = lax.rsqrt(meansq + norm_eps)
    q_sum = jnp.zeros((rows, columns), jnp.float32)
    kv_sum = jnp.zeros((rows, kv_columns), jnp.float32)
    for k in range(pieces):
        start = pl.multiple_of(lax.bitwise_xor(me, order[k]) * depth, 128)
        gain = gain_ref[:, pl.ds(start, depth)]
        normed = (shards[k][...].astype(jnp.float32) * inverse * gain).astype(jnp.bfloat16)
        kv_sum += lax.dot_general(
            normed,
            wkv_ref[:, pl.ds(start, depth)],
            (((1,), (1,)), ((), ())),
            preferred_element_type=jnp.float32,
        )
        q_sum += jnp.dot(normed, wq_ref[pl.ds(start, depth), :], preferred_element_type=jnp.float32)
    odd = lax.bitwise_and(me, 1).astype(jnp.float32)
    both = jnp.concatenate([kv_sum * (1.0 - odd), kv_sum * odd], axis=-1)
    for k in range(targets):
        take = slice(k * per_target, (k + 1) * per_target)
        out_ref[k, :, :columns] = q_sum[take].astype(jnp.bfloat16)
        out_ref[k, :, columns:] = both[take].astype(jnp.bfloat16)


def project(order, shards, norm_gain, w_query, w_keyval, mark, per_target):
    pieces = len(shards)
    rows = shards[0].shape[0]
    vmem = pl.BlockSpec(memory_space=pltpu.VMEM)
    return pl.pallas_call(
        lambda *refs: project_kernel(order, pieces, *refs),
        out_shape=jax.ShapeDtypeStruct(
            (rows // per_target, per_target, w_query.shape[1] + 2 * w_keyval.shape[0]), jnp.bfloat16
        ),
        in_specs=[vmem] * (pieces + 4),
        out_specs=vmem,
        compiler_params=pltpu.CompilerParams(vmem_limit_bytes=16 * 1024 * 1024),
        name="project",
    )(*shards, norm_gain, w_query, w_keyval, mark)


def attend_kernel(
    lengths_ref, rows_ref, cos_ref, sin_ref, kf_ref, vf_ref, keys_ref, values_ref, out_ref
):
    sources, local_rows, _ = rows_ref.shape
    span = keys_ref.shape[1]
    each = out_ref.shape[-1] // HD
    heads = each * sources
    per_key = HQ // KVH // each
    blocks = kf_ref.shape[1]
    per_block = span // blocks
    source = lax.broadcasted_iota(jnp.int32, (heads, HD), 0) % sources
    key_head = source // per_key
    pick_row = lax.broadcasted_iota(jnp.int32, (2 * sources, sources), 0)
    pick_col = lax.broadcasted_iota(jnp.int32, (2 * sources, sources), 1)
    wanted = (pick_row % sources) // per_key + KVH * (pick_row // sources)
    pick = (pick_col // 2 == wanted).astype(jnp.bfloat16)
    place = lax.broadcasted_iota(jnp.int32, (heads, span), 1)
    block_head = lax.broadcasted_iota(jnp.int32, (heads, per_block), 0) % sources // per_key

    def scaled(values, scale_ref, r):
        parts = []
        for b in range(blocks):
            scale = jnp.full((heads, per_block), scale_ref[r, b, 0])
            for k in range(1, KVH):
                scale = jnp.where(block_head == k, scale_ref[r, b, k], scale)
            parts.append(values[:, b * per_block : (b + 1) * per_block] * scale)
        return jnp.concatenate(parts, axis=1)

    for r in range(local_rows):
        got = rows_ref[:, r, :].astype(jnp.float32)
        cosine = cos_ref[r : r + 1, :]
        sine = sin_ref[r : r + 1, :]

        def turn(vec):
            return (vec * cosine + pltpu.roll(vec, HD // 2, 1) * sine).astype(jnp.bfloat16)

        query = turn(
            jnp.concatenate([got[:, g * HD : (g + 1) * HD] for g in range(each)], axis=0)
        )
        fresh = jnp.dot(
            pick, got[:, each * HD :].astype(jnp.bfloat16), preferred_element_type=jnp.float32
        )
        new_key = turn(fresh[:sources]).astype(jnp.float32)
        new_key = jnp.concatenate([new_key] * each, axis=0)
        new_value = jnp.concatenate([fresh[sources:]] * each, axis=0)
        wide = jnp.concatenate(
            [jnp.where(key_head == k, query, jnp.zeros_like(query)) for k in range(KVH)], axis=1
        )
        scores = lax.dot_general(
            wide, keys_ref[r], (((1,), (1,)), ((), ())), preferred_element_type=jnp.float32
        )
        scores = scaled(scores, kf_ref, r)
        scores = jnp.where(place < lengths_ref[r], scores * HD ** (-0.5), -jnp.inf)
        own = jnp.sum(query.astype(jnp.float32) * new_key, axis=-1, keepdims=True) * HD ** (-0.5)
        top = jnp.maximum(jnp.max(scores, axis=-1, keepdims=True), own)
        weights = jnp.exp(scores - top)
        own_weight = jnp.exp(own - top)
        total = jnp.sum(weights, axis=-1, keepdims=True) + own_weight
        rounded = weights.astype(jnp.bfloat16).astype(jnp.float32)
        rounded = scaled(rounded, vf_ref, r).astype(jnp.bfloat16)
        summed = jnp.dot(rounded, values_ref[r], preferred_element_type=jnp.float32)
        mine = summed[:, :HD]
        for k in range(1, KVH):
            mine = jnp.where(key_head == k, summed[:, k * HD : (k + 1) * HD], mine)
        mine = mine + own_weight.astype(jnp.bfloat16).astype(jnp.float32) * new_value
        mine = (mine / total).astype(jnp.bfloat16)
        for g in range(each):
            out_ref[:, r, g * HD : (g + 1) * HD] = mine[g * sources : (g + 1) * sources]


def attend(rows, columns, lengths, cosine, sine, key_factors, value_factors, key_cache, value_cache):
    sources, local_rows, _ = rows.shape
    smem = pl.BlockSpec(memory_space=pltpu.SMEM)
    vmem = pl.BlockSpec(memory_space=pltpu.VMEM)
    return pl.pallas_call(
        attend_kernel,
        out_shape=jax.ShapeDtypeStruct((sources, local_rows, columns), jnp.bfloat16),
        in_specs=[smem] + [vmem] * 3 + [smem] * 2 + [vmem] * 2,
        out_specs=vmem,
        compiler_params=pltpu.CompilerParams(vmem_limit_bytes=8 * 1024 * 1024),
        name="attend",
    )(lengths, rows, cosine, sine, key_factors, value_factors, key_cache, value_cache)


def expand_kernel(order, heads_ref, w_ref, out_ref):
    width = out_ref.shape[-1]
    me = lax.axis_index("out")
    heads = jnp.concatenate(
        [heads_ref[k].astype(jnp.float32) for k in range(heads_ref.shape[0])], axis=0
    ).astype(jnp.bfloat16)
    for k in range(len(order)):
        start = pl.multiple_of(lax.bitwise_xor(me, order[k]) * width, 128)
        out_ref[k] = jnp.dot(
            heads, w_ref[:, pl.ds(start, width)], preferred_element_type=jnp.float32
        ).astype(out_ref.dtype)


def expand(order, heads, w_out, width, dtype):
    vmem = pl.BlockSpec(memory_space=pltpu.VMEM)
    return pl.pallas_call(
        lambda *refs: expand_kernel(order, *refs),
        out_shape=jax.ShapeDtypeStruct(
            (len(order), heads.shape[0] * heads.shape[1], width), dtype
        ),
        in_specs=[vmem, vmem],
        out_specs=vmem,
        compiler_params=pltpu.CompilerParams(vmem_limit_bytes=16 * 1024 * 1024),
        name="expand",
    )(heads, w_out)


def per_device(
    size,
    stream,
    norm_gain,
    w_query,
    w_keyval,
    w_out,
    lengths,
    key_cache,
    value_cache,
    key_scales,
    value_scales,
):
    local_rows = lengths.shape[0]
    width = stream.shape[1]
    columns = w_query.shape[1]

    block = [m for m in (2, 6, 4) if m < size]
    tops = [1 << k for k in range(3, size.bit_length() - 1)]
    w_keyval = w_keyval.T
    norm_gain = norm_gain.reshape(1, -1)
    held = {0: stream}
    for bit in tops[::-1]:
        for mask in list(held):
            held[mask | bit] = swapped(held[mask], bit, size, f"gather_{mask | bit}")
    last = max(held)
    held[last], mark = lax.optimization_barrier(
        (held[last], stage(2 * 2 * (w_query.size + w_keyval.size + w_out.size) // 2))
    )
    for mask in list(held):
        for over in block:
            held[mask | over] = swapped(held[mask], over, size, f"gather_{mask | over}")
    for mask in list(held):
        held[mask | 1] = swapped(held[mask], 1, size, f"gather_{mask | 1}")
    order = list(held)
    freq = jnp.exp(
        jnp.arange(HD // 2, dtype=jnp.float32) * (-2.0 * math.log(rope_base) / HD)
    )
    angle = lengths.astype(jnp.float32)[:, None] * freq
    cosine, sine = jnp.cos(angle), jnp.sin(angle)
    side = (
        jnp.concatenate([cosine, cosine], axis=-1),
        jnp.concatenate([-sine, sine], axis=-1),
        jnp.exp2(key_scales.astype(jnp.float32)),
        jnp.exp2(value_scales.astype(jnp.float32)),
    )
    side, held[size - 1] = lax.optimization_barrier((side, held[size - 1]))
    qkv = project(order, [held[m] for m in order], norm_gain, w_query, w_keyval, mark, local_rows)
    rows = lax.all_to_all(qkv, "out", split_axis=0, concat_axis=0, tiled=True)
    attended = attend(rows, columns, lengths, *side, key_cache, value_cache)
    heads = lax.all_to_all(attended, "out", split_axis=0, concat_axis=0, tiled=True)

    owed = {}
    spans = [t for t in range(0, size, 8)][::-1]
    for top in spans:
        near = [top | m for m in block + [0]]
        away = [m | 1 for m in near]
        sent = expand(away, heads, w_out, width, jnp.bfloat16)
        sent = swapped(sent, 1, size, f"scatter_{top | 1}")
        kept = expand(near, heads, w_out, width, jnp.float32)
        for k, mask in enumerate(near):
            owed[mask] = kept[k] + sent[k].astype(jnp.float32)
        for mask in near[:-1]:
            got = swapped(owed[mask].astype(jnp.bfloat16), mask ^ top, size, f"scatter_{mask}")
            owed[top] = owed[top] + got.astype(jnp.float32)
    for bit in tops[::-1]:
        for mask in [m for m in spans if m & bit and m < 2 * bit]:
            got = swapped(owed[mask].astype(jnp.bfloat16), bit, size, f"scatter_{mask}")
            owed[mask ^ bit] = owed[mask ^ bit] + got.astype(jnp.float32)
    return (stream.astype(jnp.float32) + owed[0]).astype(jnp.bfloat16)


def solution(mesh):
    size = mesh.shape["out"]

    def step(stream, *rest):
        columns = rest[1].shape[1]
        whole_heads = columns % HD == 0 and HQ // KVH * HD % columns == 0 and 2 * rest[2].shape[1] == HD
        if size & (size - 1) == 0 and stream.shape[1] % 128 == 0 and whole_heads:
            return per_device(size, stream, *rest)
        return per_device_general(stream, *rest)

    return jax.shard_map(
        step,
        mesh=mesh,
        in_specs=(
            P("groups", "out"),
            P(),
            P(None, "out"),
            P(None, "out"),
            P("out", None),
            P(("groups", "out")),
            P(("groups", "out"), None, None),
            P(("groups", "out"), None, None),
            P(("groups", "out"), None, None),
            P(("groups", "out"), None, None),
        ),
        out_specs=P("groups", "out"),
        check_vma=False,
    )
```

```python
import math

import jax
import jax.numpy as jnp
from jax import lax
from jax.experimental import pallas as pl
from jax.experimental.pallas import tpu as pltpu
from jax.sharding import PartitionSpec as P

HQ = 48
KVH = 4
HD = 128


rope_base = 1000000.0
norm_eps = 1e-05


def rotate(vec, position):
    half = vec.shape[-1] // 2
    index = jnp.arange(half, dtype=jnp.float32)
    freq = jnp.exp(index * (-2.0 * math.log(rope_base) / vec.shape[-1]))
    angle = position * freq
    cosine = jnp.cos(angle)
    sine = jnp.sin(angle)
    first = vec[..., :half]
    second = vec[..., half:]
    return jnp.concatenate(
        [first * cosine - second * sine, second * cosine + first * sine], axis=-1
    )


def dequant(cache, scales):
    rows, span, width = cache.shape
    blocks = scales.shape[1]
    factor = jnp.exp2(scales.astype(jnp.float32)).astype(jnp.bfloat16)
    shaped = cache.reshape(rows, blocks, span // blocks, KVH, width // KVH)
    return (shaped * factor[:, :, None, :, None]).reshape(rows, span, KVH, width // KVH)


def per_device_general(
    stream,
    norm_gain,
    w_query,
    w_keyval,
    w_out,
    lengths,
    key_cache,
    value_cache,
    key_scales,
    value_scales,
):
    local_rows = lengths.shape[0]
    xf = stream.astype(jnp.float32)
    whole = lax.all_gather(stream, "out", axis=1, tiled=True).astype(jnp.float32)
    meansq = jnp.mean(whole * whole, axis=-1, keepdims=True)
    normed = (whole * lax.rsqrt(meansq + norm_eps) * norm_gain).astype(jnp.bfloat16)
    q_local = jnp.dot(normed, w_query, preferred_element_type=jnp.float32).astype(jnp.bfloat16)
    kv_local = jnp.dot(normed, w_keyval, preferred_element_type=jnp.float32).astype(jnp.bfloat16)
    q_rows, kv_rows = (
        lax.all_to_all(q_local, "out", split_axis=0, concat_axis=1, tiled=True),
        lax.all_to_all(kv_local, "out", split_axis=0, concat_axis=1, tiled=True),
    )
    position = lengths.astype(jnp.float32)[:, None, None]
    rotated = rotate(q_rows.astype(jnp.float32).reshape(local_rows, HQ, HD), position).astype(
        jnp.bfloat16
    )
    rotated = rotated.reshape(local_rows, KVH, HQ // KVH, HD)
    new_key = rotate(
        kv_rows[:, : KVH * HD].astype(jnp.float32).reshape(local_rows, KVH, HD), position
    ).astype(jnp.bfloat16)
    new_value = kv_rows[:, KVH * HD :].reshape(local_rows, KVH, HD)
    factor = HD ** (-0.5)
    own = jnp.einsum("rkgd,rkd->rkg", rotated, new_key, preferred_element_type=jnp.float32) * factor
    span = key_cache.shape[1]
    scores = (
        jnp.einsum(
            "rkgd,rjkd->rkgj",
            rotated,
            dequant(key_cache, key_scales),
            preferred_element_type=jnp.float32,
        )
        * factor
    )
    valid = jnp.arange(span, dtype=jnp.int32)[None, :] < lengths[:, None]
    scores = jnp.where(valid[:, None, None, :], scores, -jnp.inf)
    top = jnp.maximum(jnp.max(scores, axis=-1), own)
    weights = jnp.exp(scores - top[..., None])
    own_weight = jnp.exp(own - top)
    total = jnp.sum(weights, axis=-1) + own_weight
    own_rounded = lax.optimization_barrier(own_weight.astype(jnp.bfloat16)).astype(jnp.float32)
    summed = jnp.einsum(
        "rkgj,rjkd->rkgd",
        weights.astype(jnp.bfloat16),
        dequant(value_cache, value_scales),
        preferred_element_type=jnp.float32,
    )
    summed = summed + own_rounded[..., None] * new_value.astype(jnp.float32)[:, :, None, :]
    attended = (summed / total[..., None]).astype(jnp.bfloat16).reshape(local_rows, HQ * HD)
    heads = lax.all_to_all(attended, "out", split_axis=1, concat_axis=0, tiled=True)
    partial_terms = jnp.dot(heads, w_out, preferred_element_type=jnp.float32)
    projected = lax.psum_scatter(partial_terms, "out", scatter_dimension=1, tiled=True)
    return (xf + projected).astype(jnp.bfloat16)


def swapped(value, mask, size, label):
    with jax.named_scope(label):
        return lax.ppermute(value, "out", [(i, i ^ mask) for i in range(size)])


def room_kernel(out_ref):
    pass


def stage_kernel(*refs):
    refs[-1][...] = jnp.zeros_like(refs[-1])


def stage(cover):
    vmem = pl.BlockSpec(memory_space=pltpu.VMEM)
    small = pltpu.CompilerParams(vmem_limit_bytes=2 * 1024 * 1024)
    room = pl.pallas_call(
        room_kernel,
        out_shape=jax.ShapeDtypeStruct((2048, 512), jnp.bfloat16),
        out_specs=vmem,
        compiler_params=small,
        name="room",
    )()
    count = -(-cover // (2 * room.size))
    return pl.pallas_call(
        stage_kernel,
        out_shape=jax.ShapeDtypeStruct((8, 128), jnp.float32),
        in_specs=[pl.BlockSpec(memory_space=pl.ANY)] * count,
        out_specs=vmem,
        compiler_params=small,
        name="stage",
    )(*[room] * count)


def project_kernel(order, pieces, *refs):
    shards = refs[:pieces]
    gain_ref, wq_ref, wkv_ref, _, out_ref = refs[pieces:]
    rows, depth = shards[0].shape
    columns, kv_columns = wq_ref.shape[1], wkv_ref.shape[0]
    targets, per_target, _ = out_ref.shape
    me = lax.axis_index("out")
    square = jnp.zeros((rows, 128), jnp.float32)
    for k in range(pieces):
        part = shards[k][...].astype(jnp.float32)
        part = part * part
        for lane in range(0, depth, 128):
            square += part[:, lane : lane + 128]
    meansq = jnp.sum(square, axis=-1, keepdims=True) / (depth * pieces)
    inverse = lax.rsqrt(meansq + norm_eps)
    q_sum = jnp.zeros((rows, columns), jnp.float32)
    kv_sum = jnp.zeros((rows, kv_columns), jnp.float32)
    for k in range(pieces):
        start = pl.multiple_of(lax.bitwise_xor(me, order[k]) * depth, 128)
        gain = gain_ref[:, pl.ds(start, depth)]
        normed = (shards[k][...].astype(jnp.float32) * inverse * gain).astype(jnp.bfloat16)
        kv_sum += lax.dot_general(
            normed,
            wkv_ref[:, pl.ds(start, depth)],
            (((1,), (1,)), ((), ())),
            preferred_element_type=jnp.float32,
        )
        q_sum += jnp.dot(normed, wq_ref[pl.ds(start, depth), :], preferred_element_type=jnp.float32)
    odd = lax.bitwise_and(me, 1).astype(jnp.float32)
    both = jnp.concatenate([kv_sum * (1.0 - odd), kv_sum * odd], axis=-1)
    for k in range(targets):
        take = slice(k * per_target, (k + 1) * per_target)
        out_ref[k, :, :columns] = q_sum[take].astype(jnp.bfloat16)
        out_ref[k, :, columns:] = both[take].astype(jnp.bfloat16)


def project(order, shards, norm_gain, w_query, w_keyval, mark, per_target):
    pieces = len(shards)
    rows = shards[0].shape[0]
    vmem = pl.BlockSpec(memory_space=pltpu.VMEM)
    return pl.pallas_call(
        lambda *refs: project_kernel(order, pieces, *refs),
        out_shape=jax.ShapeDtypeStruct(
            (rows // per_target, per_target, w_query.shape[1] + 2 * w_keyval.shape[0]), jnp.bfloat16
        ),
        in_specs=[vmem] * (pieces + 4),
        out_specs=vmem,
        compiler_params=pltpu.CompilerParams(vmem_limit_bytes=16 * 1024 * 1024),
        name="project",
    )(*shards, norm_gain, w_query, w_keyval, mark)


def attend_kernel(
    lengths_ref, rows_ref, cos_ref, sin_ref, kf_ref, vf_ref, keys_ref, values_ref, out_ref
):
    sources, local_rows, _ = rows_ref.shape
    span = keys_ref.shape[1]
    each = out_ref.shape[-1] // HD
    heads = each * sources
    per_key = HQ // KVH // each
    blocks = kf_ref.shape[1]
    per_block = span // blocks
    each_row = range(local_rows)
    key_head = lax.broadcasted_iota(jnp.int32, (heads, HD), 0) % sources // per_key
    block_head = lax.broadcasted_iota(jnp.int32, (sources, per_block), 0) // per_key
    pick_row = lax.broadcasted_iota(jnp.int32, (2 * sources, sources), 0)
    pick_col = lax.broadcasted_iota(jnp.int32, (2 * sources, sources), 1)
    wanted = (pick_row % sources) // per_key + KVH * (pick_row // sources)
    pick = (pick_col // 2 == wanted).astype(jnp.bfloat16)
    place = lax.broadcasted_iota(jnp.int32, (heads, span), 1)

    def scaled(values, scale_ref, r):
        parts = []
        for b in range(blocks):
            scale = jnp.full((sources, per_block), scale_ref[r, b, 0])
            for k in range(1, KVH):
                scale = jnp.where(block_head == k, scale_ref[r, b, k], scale)
            scale = jnp.concatenate([scale] * each, axis=0)
            parts.append(values[:, b * per_block : (b + 1) * per_block] * scale)
        return jnp.concatenate(parts, axis=1)

    def turn(vec, r):
        cosine, sine = cos_ref[r : r + 1, :], sin_ref[r : r + 1, :]
        turned = vec * cosine + pltpu.roll(vec, HD // 2, 1) * sine
        return turned.astype(jnp.bfloat16).astype(jnp.float32)

    got = [rows_ref[:, r, :].astype(jnp.float32) for r in each_row]
    fresh = jnp.dot(
        pick,
        jnp.concatenate([g[:, each * HD :] for g in got], axis=1).astype(jnp.bfloat16),
        preferred_element_type=jnp.float32,
    )
    query, scores = [], []
    for r in each_row:
        query.append(
            turn(
                jnp.concatenate([got[r][:, g * HD : (g + 1) * HD] for g in range(each)], axis=0), r
            )
        )
        wide = jnp.concatenate(
            [jnp.where(key_head == k, query[r], 0.0) for k in range(KVH)], axis=1
        ).astype(jnp.bfloat16)
        scores.append(
            lax.dot_general(
                wide, keys_ref[r], (((1,), (1,)), ((), ())), preferred_element_type=jnp.float32
            )
        )
    own_weight, total, summed = [], [], []
    for r in each_row:
        new_key = turn(fresh[:sources, r * HD : (r + 1) * HD], r)
        new_key = jnp.concatenate([new_key] * each, axis=0)
        own = jnp.sum(query[r] * new_key, axis=-1, keepdims=True) * HD ** (-0.5)
        score = scaled(scores[r], kf_ref, r) * HD ** (-0.5)
        score = jnp.where(place < lengths_ref[r], score, -jnp.inf)
        top = jnp.maximum(jnp.max(score, axis=-1, keepdims=True), own)
        weights = jnp.exp(score - top)
        own_weight.append(jnp.exp(own - top))
        total.append(jnp.sum(weights, axis=-1, keepdims=True) + own_weight[r])
        rounded = scaled(weights.astype(jnp.bfloat16).astype(jnp.float32), vf_ref, r)
        summed.append(
            jnp.dot(
                rounded.astype(jnp.bfloat16), values_ref[r], preferred_element_type=jnp.float32
            )
        )
    for r in each_row:
        mine = summed[r][:, :HD]
        for k in range(1, KVH):
            mine = jnp.where(key_head == k, summed[r][:, k * HD : (k + 1) * HD], mine)
        new_value = jnp.concatenate([fresh[sources:, r * HD : (r + 1) * HD]] * each, axis=0)
        mine = mine + own_weight[r].astype(jnp.bfloat16).astype(jnp.float32) * new_value
        mine = (mine / total[r]).astype(jnp.bfloat16)
        for g in range(each):
            out_ref[:, r, g * HD : (g + 1) * HD] = mine[g * sources : (g + 1) * sources]


def attend(rows, columns, lengths, cosine, sine, key_factors, value_factors, key_cache, value_cache):
    sources, local_rows, _ = rows.shape
    smem = pl.BlockSpec(memory_space=pltpu.SMEM)
    vmem = pl.BlockSpec(memory_space=pltpu.VMEM)
    return pl.pallas_call(
        attend_kernel,
        out_shape=jax.ShapeDtypeStruct((sources, local_rows, columns), jnp.bfloat16),
        in_specs=[smem] + [vmem] * 3 + [smem] * 2 + [vmem] * 2,
        out_specs=vmem,
        compiler_params=pltpu.CompilerParams(vmem_limit_bytes=8 * 1024 * 1024),
        name="attend",
    )(lengths, rows, cosine, sine, key_factors, value_factors, key_cache, value_cache)


def expand_kernel(order, heads_ref, w_ref, out_ref):
    width = out_ref.shape[-1]
    me = lax.axis_index("out")
    heads = jnp.concatenate(
        [heads_ref[k].astype(jnp.float32) for k in range(heads_ref.shape[0])], axis=0
    ).astype(jnp.bfloat16)
    for k in range(len(order)):
        start = pl.multiple_of(lax.bitwise_xor(me, order[k]) * width, 128)
        out_ref[k] = jnp.dot(
            heads, w_ref[:, pl.ds(start, width)], preferred_element_type=jnp.float32
        ).astype(out_ref.dtype)


def expand(order, heads, w_out, width, dtype):
    vmem = pl.BlockSpec(memory_space=pltpu.VMEM)
    return pl.pallas_call(
        lambda *refs: expand_kernel(order, *refs),
        out_shape=jax.ShapeDtypeStruct(
            (len(order), heads.shape[0] * heads.shape[1], width), dtype
        ),
        in_specs=[vmem, vmem],
        out_specs=vmem,
        compiler_params=pltpu.CompilerParams(vmem_limit_bytes=16 * 1024 * 1024),
        name="expand",
    )(heads, w_out)


def per_device(
    size,
    stream,
    norm_gain,
    w_query,
    w_keyval,
    w_out,
    lengths,
    key_cache,
    value_cache,
    key_scales,
    value_scales,
):
    local_rows = lengths.shape[0]
    width = stream.shape[1]
    columns = w_query.shape[1]

    block = [m for m in (2, 6, 4) if m < size]
    tops = [1 << k for k in range(3, size.bit_length() - 1)]
    w_keyval = w_keyval.T
    norm_gain = norm_gain.reshape(1, -1)
    held = {0: stream}
    for bit in tops[::-1]:
        for mask in list(held):
            held[mask | bit] = swapped(held[mask], bit, size, f"gather_{mask | bit}")
    last = max(held)
    held[last], mark = lax.optimization_barrier(
        (held[last], stage(2 * 2 * (w_query.size + w_keyval.size + w_out.size) // 2))
    )
    for mask in list(held):
        for over in block:
            held[mask | over] = swapped(held[mask], over, size, f"gather_{mask | over}")
    for mask in list(held):
        held[mask | 1] = swapped(held[mask], 1, size, f"gather_{mask | 1}")
    order = list(held)
    freq = jnp.exp(
        jnp.arange(HD // 2, dtype=jnp.float32) * (-2.0 * math.log(rope_base) / HD)
    )
    angle = lengths.astype(jnp.float32)[:, None] * freq
    cosine, sine = jnp.cos(angle), jnp.sin(angle)
    side = (
        jnp.concatenate([cosine, cosine], axis=-1),
        jnp.concatenate([-sine, sine], axis=-1),
        jnp.exp2(key_scales.astype(jnp.float32)),
        jnp.exp2(value_scales.astype(jnp.float32)),
    )
    side, held[size - 1] = lax.optimization_barrier((side, held[size - 1]))
    qkv = project(order, [held[m] for m in order], norm_gain, w_query, w_keyval, mark, local_rows)
    rows = lax.all_to_all(qkv, "out", split_axis=0, concat_axis=0, tiled=True)
    attended = attend(rows, columns, lengths, *side, key_cache, value_cache)
    heads = lax.all_to_all(attended, "out", split_axis=0, concat_axis=0, tiled=True)

    owed = {}
    spans = [t for t in range(0, size, 8)][::-1]
    for top in spans:
        near = [top | m for m in block + [0]]
        away = [m | 1 for m in near]
        sent = expand(away, heads, w_out, width, jnp.bfloat16)
        sent = swapped(sent, 1, size, f"scatter_{top | 1}")
        kept = expand(near, heads, w_out, width, jnp.float32)
        for k, mask in enumerate(near):
            owed[mask] = kept[k] + sent[k].astype(jnp.float32)
        for mask in near[:-1]:
            got = swapped(owed[mask].astype(jnp.bfloat16), mask ^ top, size, f"scatter_{mask}")
            owed[top] = owed[top] + got.astype(jnp.float32)
    for bit in tops[::-1]:
        for mask in [m for m in spans if m & bit and m < 2 * bit]:
            got = swapped(owed[mask].astype(jnp.bfloat16), bit, size, f"scatter_{mask}")
            owed[mask ^ bit] = owed[mask ^ bit] + got.astype(jnp.float32)
    return (stream.astype(jnp.float32) + owed[0]).astype(jnp.bfloat16)


def solution(mesh):
    size = mesh.shape["out"]

    def step(stream, *rest):
        columns = rest[1].shape[1]
        whole_heads = columns % HD == 0 and HQ // KVH * HD % columns == 0 and 2 * rest[2].shape[1] == HD
        if size & (size - 1) == 0 and stream.shape[1] % 128 == 0 and whole_heads:
            return per_device(size, stream, *rest)
        return per_device_general(stream, *rest)

    return jax.shard_map(
        step,
        mesh=mesh,
        in_specs=(
            P("groups", "out"),
            P(),
            P(None, "out"),
            P(None, "out"),
            P("out", None),
            P(("groups", "out")),
            P(("groups", "out"), None, None),
            P(("groups", "out"), None, None),
            P(("groups", "out"), None, None),
            P(("groups", "out"), None, None),
        ),
        out_specs=P("groups", "out"),
        check_vma=False,
    )
```

```python
import math

import jax
import jax.numpy as jnp
from jax import lax
from jax.experimental import pallas as pl
from jax.experimental.pallas import tpu as pltpu
from jax.sharding import PartitionSpec as P


HQ = 48
KVH = 4
HD = 128


rope_base = 1000000.0
norm_eps = 1e-05


def rotate(vec, position):
    half = vec.shape[-1] // 2
    index = jnp.arange(half, dtype=jnp.float32)
    freq = jnp.exp(index * (-2.0 * math.log(rope_base) / vec.shape[-1]))
    angle = position * freq
    cosine = jnp.cos(angle)
    sine = jnp.sin(angle)
    first = vec[..., :half]
    second = vec[..., half:]
    return jnp.concatenate(
        [first * cosine - second * sine, second * cosine + first * sine], axis=-1
    )


def dequant(cache, scales):
    rows, span, width = cache.shape
    blocks = scales.shape[1]
    factor = jnp.exp2(scales.astype(jnp.float32)).astype(jnp.bfloat16)
    shaped = cache.reshape(rows, blocks, span // blocks, KVH, width // KVH)
    return (shaped * factor[:, :, None, :, None]).reshape(rows, span, KVH, width // KVH)


def per_device_general(
    stream,
    norm_gain,
    w_query,
    w_keyval,
    w_out,
    lengths,
    key_cache,
    value_cache,
    key_scales,
    value_scales,
):
    local_rows = lengths.shape[0]
    xf = stream.astype(jnp.float32)
    whole = lax.all_gather(stream, "out", axis=1, tiled=True).astype(jnp.float32)
    meansq = jnp.mean(whole * whole, axis=-1, keepdims=True)
    normed = (whole * lax.rsqrt(meansq + norm_eps) * norm_gain).astype(jnp.bfloat16)
    q_local = jnp.dot(normed, w_query, preferred_element_type=jnp.float32).astype(jnp.bfloat16)
    kv_local = jnp.dot(normed, w_keyval, preferred_element_type=jnp.float32).astype(jnp.bfloat16)
    q_rows, kv_rows = (
        lax.all_to_all(q_local, "out", split_axis=0, concat_axis=1, tiled=True),
        lax.all_to_all(kv_local, "out", split_axis=0, concat_axis=1, tiled=True),
    )
    position = lengths.astype(jnp.float32)[:, None, None]
    rotated = rotate(q_rows.astype(jnp.float32).reshape(local_rows, HQ, HD), position).astype(
        jnp.bfloat16
    )
    rotated = rotated.reshape(local_rows, KVH, HQ // KVH, HD)
    new_key = rotate(
        kv_rows[:, : KVH * HD].astype(jnp.float32).reshape(local_rows, KVH, HD), position
    ).astype(jnp.bfloat16)
    new_value = kv_rows[:, KVH * HD :].reshape(local_rows, KVH, HD)
    factor = HD ** (-0.5)
    own = jnp.einsum("rkgd,rkd->rkg", rotated, new_key, preferred_element_type=jnp.float32) * factor
    span = key_cache.shape[1]
    scores = (
        jnp.einsum(
            "rkgd,rjkd->rkgj",
            rotated,
            dequant(key_cache, key_scales),
            preferred_element_type=jnp.float32,
        )
        * factor
    )
    valid = jnp.arange(span, dtype=jnp.int32)[None, :] < lengths[:, None]
    scores = jnp.where(valid[:, None, None, :], scores, -jnp.inf)
    top = jnp.maximum(jnp.max(scores, axis=-1), own)
    weights = jnp.exp(scores - top[..., None])
    own_weight = jnp.exp(own - top)
    total = jnp.sum(weights, axis=-1) + own_weight
    own_rounded = lax.optimization_barrier(own_weight.astype(jnp.bfloat16)).astype(jnp.float32)
    summed = jnp.einsum(
        "rkgj,rjkd->rkgd",
        weights.astype(jnp.bfloat16),
        dequant(value_cache, value_scales),
        preferred_element_type=jnp.float32,
    )
    summed = summed + own_rounded[..., None] * new_value.astype(jnp.float32)[:, :, None, :]
    attended = (summed / total[..., None]).astype(jnp.bfloat16).reshape(local_rows, HQ * HD)
    heads = lax.all_to_all(attended, "out", split_axis=1, concat_axis=0, tiled=True)
    partial_terms = jnp.dot(heads, w_out, preferred_element_type=jnp.float32)
    projected = lax.psum_scatter(partial_terms, "out", scatter_dimension=1, tiled=True)
    return (xf + projected).astype(jnp.bfloat16)


def swapped(value, mask, size):
    return lax.ppermute(value, "out", [(i, i ^ mask) for i in range(size)])


def room_kernel(out_ref):
    pass


def stage_kernel(*refs):
    refs[-1][...] = jnp.zeros_like(refs[-1])


def stage(cover):
    vmem = pl.BlockSpec(memory_space=pltpu.VMEM)
    small = pltpu.CompilerParams(vmem_limit_bytes=2 * 1024 * 1024)
    room = pl.pallas_call(
        room_kernel,
        out_shape=jax.ShapeDtypeStruct((2048, 512), jnp.bfloat16),
        out_specs=vmem,
        compiler_params=small,
        name="room",
    )()
    count = -(-cover // (2 * room.size))
    return pl.pallas_call(
        stage_kernel,
        out_shape=jax.ShapeDtypeStruct((8, 128), jnp.float32),
        in_specs=[pl.BlockSpec(memory_space=pl.ANY)] * count,
        out_specs=vmem,
        compiler_params=small,
        name="stage",
    )(*[room] * count)


def project_kernel(order, pieces, *refs):
    shards = refs[:pieces]
    gain_ref, wq_ref, wkv_ref, _, out_ref = refs[pieces:]
    rows, depth = shards[0].shape
    columns, kv_columns = wq_ref.shape[1], wkv_ref.shape[0]
    targets, per_target, _ = out_ref.shape
    me = lax.axis_index("out")
    square = jnp.zeros((rows, 128), jnp.float32)
    for k in range(pieces):
        part = shards[k][...].astype(jnp.float32)
        part = part * part
        for lane in range(0, depth, 128):
            square += part[:, lane : lane + 128]
    meansq = jnp.sum(square, axis=-1, keepdims=True) / (depth * pieces)
    inverse = lax.rsqrt(meansq + norm_eps)
    q_sum = jnp.zeros((rows, columns), jnp.float32)
    kv_sum = jnp.zeros((rows, kv_columns), jnp.float32)
    for k in range(pieces):
        start = pl.multiple_of(lax.bitwise_xor(me, order[k]) * depth, 128)
        gain = gain_ref[:, pl.ds(start, depth)]
        normed = (shards[k][...].astype(jnp.float32) * inverse * gain).astype(jnp.bfloat16)
        kv_sum += lax.dot_general(
            normed,
            wkv_ref[:, pl.ds(start, depth)],
            (((1,), (1,)), ((), ())),
            preferred_element_type=jnp.float32,
        )
        q_sum += jnp.dot(normed, wq_ref[pl.ds(start, depth), :], preferred_element_type=jnp.float32)
    odd = lax.bitwise_and(me, 1).astype(jnp.float32)
    both = jnp.concatenate([kv_sum * (1.0 - odd), kv_sum * odd], axis=-1)
    for k in range(targets):
        take = slice(k * per_target, (k + 1) * per_target)
        out_ref[k, :, :columns] = q_sum[take].astype(jnp.bfloat16)
        out_ref[k, :, columns:] = both[take].astype(jnp.bfloat16)


def project(order, shards, norm_gain, w_query, w_keyval, mark, per_target):
    pieces = len(shards)
    rows = shards[0].shape[0]
    vmem = pl.BlockSpec(memory_space=pltpu.VMEM)
    return pl.pallas_call(
        lambda *refs: project_kernel(order, pieces, *refs),
        out_shape=jax.ShapeDtypeStruct(
            (rows // per_target, per_target, w_query.shape[1] + 2 * w_keyval.shape[0]), jnp.bfloat16
        ),
        in_specs=[vmem] * (pieces + 4),
        out_specs=vmem,
        compiler_params=pltpu.CompilerParams(vmem_limit_bytes=16 * 1024 * 1024),
        name="project",
    )(*shards, norm_gain, w_query, w_keyval, mark)


def attend_kernel(
    lengths_ref, rows_ref, cos_ref, sin_ref, kf_ref, vf_ref, keys_ref, values_ref, out_ref
):
    sources, local_rows, _ = rows_ref.shape
    span = keys_ref.shape[1]
    each = out_ref.shape[-1] // HD
    heads = each * sources
    per_key = HQ // KVH // each
    blocks = kf_ref.shape[1]
    per_block = span // blocks
    each_row = range(local_rows)
    key_head = lax.broadcasted_iota(jnp.int32, (heads, HD), 0) % sources // per_key
    block_head = lax.broadcasted_iota(jnp.int32, (sources, per_block), 0) // per_key
    pick_row = lax.broadcasted_iota(jnp.int32, (2 * sources, sources), 0)
    pick_col = lax.broadcasted_iota(jnp.int32, (2 * sources, sources), 1)
    wanted = (pick_row % sources) // per_key + KVH * (pick_row // sources)
    pick = (pick_col // 2 == wanted).astype(jnp.bfloat16)
    place = lax.broadcasted_iota(jnp.int32, (heads, span), 1)

    def scaled(values, scale_ref, r):
        parts = []
        for b in range(blocks):
            scale = jnp.full((sources, per_block), scale_ref[r, b, 0])
            for k in range(1, KVH):
                scale = jnp.where(block_head == k, scale_ref[r, b, k], scale)
            scale = jnp.concatenate([scale] * each, axis=0)
            parts.append(values[:, b * per_block : (b + 1) * per_block] * scale)
        return jnp.concatenate(parts, axis=1)

    def turn(vec, r):
        cosine, sine = cos_ref[r : r + 1, :], sin_ref[r : r + 1, :]
        turned = vec * cosine + pltpu.roll(vec, HD // 2, 1) * sine
        return turned.astype(jnp.bfloat16).astype(jnp.float32)

    got = [rows_ref[:, r, :].astype(jnp.float32) for r in each_row]
    fresh = jnp.dot(
        pick,
        jnp.concatenate([g[:, each * HD :] for g in got], axis=1).astype(jnp.bfloat16),
        preferred_element_type=jnp.float32,
    )
    query, scores = [], []
    for r in each_row:
        query.append(
            turn(
                jnp.concatenate([got[r][:, g * HD : (g + 1) * HD] for g in range(each)], axis=0), r
            )
        )
        wide = jnp.concatenate(
            [jnp.where(key_head == k, query[r], 0.0) for k in range(KVH)], axis=1
        ).astype(jnp.bfloat16)
        scores.append(
            lax.dot_general(
                wide, keys_ref[r], (((1,), (1,)), ((), ())), preferred_element_type=jnp.float32
            )
        )
    own_weight, total, summed = [], [], []
    for r in each_row:
        new_key = turn(fresh[:sources, r * HD : (r + 1) * HD], r)
        new_key = jnp.concatenate([new_key] * each, axis=0)
        own = jnp.sum(query[r] * new_key, axis=-1, keepdims=True) * HD ** (-0.5)
        score = scaled(scores[r], kf_ref, r) * HD ** (-0.5)
        score = jnp.where(place < lengths_ref[r], score, -jnp.inf)
        top = jnp.maximum(jnp.max(score, axis=-1, keepdims=True), own)
        weights = jnp.exp(score - top)
        own_weight.append(jnp.exp(own - top))
        total.append(jnp.sum(weights, axis=-1, keepdims=True) + own_weight[r])
        rounded = scaled(weights.astype(jnp.bfloat16).astype(jnp.float32), vf_ref, r)
        summed.append(
            jnp.dot(
                rounded.astype(jnp.bfloat16), values_ref[r], preferred_element_type=jnp.float32
            )
        )
    for r in each_row:
        mine = summed[r][:, :HD]
        for k in range(1, KVH):
            mine = jnp.where(key_head == k, summed[r][:, k * HD : (k + 1) * HD], mine)
        new_value = jnp.concatenate([fresh[sources:, r * HD : (r + 1) * HD]] * each, axis=0)
        mine = mine + own_weight[r].astype(jnp.bfloat16).astype(jnp.float32) * new_value
        mine = (mine / total[r]).astype(jnp.bfloat16)
        for g in range(each):
            out_ref[:, r, g * HD : (g + 1) * HD] = mine[g * sources : (g + 1) * sources]


def attend(rows, columns, lengths, cosine, sine, key_factors, value_factors, key_cache, value_cache):
    sources, local_rows, _ = rows.shape
    smem = pl.BlockSpec(memory_space=pltpu.SMEM)
    vmem = pl.BlockSpec(memory_space=pltpu.VMEM)
    return pl.pallas_call(
        attend_kernel,
        out_shape=jax.ShapeDtypeStruct((sources, local_rows, columns), jnp.bfloat16),
        in_specs=[smem] + [vmem] * 3 + [smem] * 2 + [vmem] * 2,
        out_specs=vmem,
        compiler_params=pltpu.CompilerParams(vmem_limit_bytes=8 * 1024 * 1024),
        name="attend",
    )(lengths, rows, cosine, sine, key_factors, value_factors, key_cache, value_cache)


def expand_kernel(order, heads_ref, w_ref, out_ref):
    width = out_ref.shape[-1]
    me = lax.axis_index("out")
    heads = jnp.concatenate(
        [heads_ref[k].astype(jnp.float32) for k in range(heads_ref.shape[0])], axis=0
    ).astype(jnp.bfloat16)
    for k in range(len(order)):
        start = pl.multiple_of(lax.bitwise_xor(me, order[k]) * width, 128)
        out_ref[k] = jnp.dot(
            heads, w_ref[:, pl.ds(start, width)], preferred_element_type=jnp.float32
        ).astype(out_ref.dtype)


def expand(order, heads, w_out, width, dtype):
    vmem = pl.BlockSpec(memory_space=pltpu.VMEM)
    return pl.pallas_call(
        lambda *refs: expand_kernel(order, *refs),
        out_shape=jax.ShapeDtypeStruct(
            (len(order), heads.shape[0] * heads.shape[1], width), dtype
        ),
        in_specs=[vmem, vmem],
        out_specs=vmem,
        compiler_params=pltpu.CompilerParams(vmem_limit_bytes=16 * 1024 * 1024),
        name="expand",
    )(heads, w_out)


def per_device(
    size,
    stream,
    norm_gain,
    w_query,
    w_keyval,
    w_out,
    lengths,
    key_cache,
    value_cache,
    key_scales,
    value_scales,
):
    local_rows = lengths.shape[0]
    width = stream.shape[1]
    columns = w_query.shape[1]

    block = [m for m in (2, 4, 6) if m < size]
    tops = [1 << k for k in range(3, size.bit_length() - 1)]
    w_keyval = w_keyval.T
    norm_gain = norm_gain.reshape(1, -1)
    held = {0: stream}
    for bit in tops[::-1]:
        for mask in list(held):
            held[mask | bit] = swapped(held[mask], bit, size)
    last = max(held)
    held[last], mark = lax.optimization_barrier(
        (held[last], stage(2 * (w_query.size + w_keyval.size + w_out.size)))
    )
    for mask in list(held):
        for over in block:
            held[mask | over] = swapped(held[mask], over, size)
    for mask in list(held):
        held[mask | 1] = swapped(held[mask], 1, size)
    order = list(held)
    freq = jnp.exp(
        jnp.arange(HD // 2, dtype=jnp.float32) * (-2.0 * math.log(rope_base) / HD)
    )
    angle = lengths.astype(jnp.float32)[:, None] * freq
    cosine, sine = jnp.cos(angle), jnp.sin(angle)
    side = (
        jnp.concatenate([cosine, cosine], axis=-1),
        jnp.concatenate([-sine, sine], axis=-1),
        jnp.exp2(key_scales.astype(jnp.float32)),
        jnp.exp2(value_scales.astype(jnp.float32)),
    )
    side, held[size - 1] = lax.optimization_barrier((side, held[size - 1]))
    qkv = project(order, [held[m] for m in order], norm_gain, w_query, w_keyval, mark, local_rows)
    rows = lax.all_to_all(qkv, "out", split_axis=0, concat_axis=0, tiled=True)
    attended = attend(rows, columns, lengths, *side, key_cache, value_cache)
    heads = lax.all_to_all(attended, "out", split_axis=0, concat_axis=0, tiled=True)

    owed = {}
    spans = [t for t in range(0, size, 8)][::-1]
    for top in spans:
        near = [top | m for m in block + [0]]
        away = [m | 1 for m in near]
        sent = expand(away, heads, w_out, width, jnp.bfloat16)
        sent = swapped(sent, 1, size)
        kept = expand(near, heads, w_out, width, jnp.float32)
        for k, mask in enumerate(near):
            owed[mask] = kept[k] + sent[k].astype(jnp.float32)
        for mask in near[-2::-1]:
            got = swapped(owed[mask].astype(jnp.bfloat16), mask ^ top, size)
            owed[top] = owed[top] + got.astype(jnp.float32)
    for bit in tops[::-1]:
        for mask in [m for m in spans if m & bit and m < 2 * bit]:
            got = swapped(owed[mask].astype(jnp.bfloat16), bit, size)
            owed[mask ^ bit] = owed[mask ^ bit] + got.astype(jnp.float32)
    return (stream.astype(jnp.float32) + owed[0]).astype(jnp.bfloat16)


def solution(mesh):
    size = mesh.shape["out"]

    def step(stream, *rest):
        columns = rest[1].shape[1]
        whole_heads = columns % HD == 0 and HQ // KVH * HD % columns == 0 and 2 * rest[2].shape[1] == HD
        if size & (size - 1) == 0 and stream.shape[1] % 128 == 0 and whole_heads:
            return per_device(size, stream, *rest)
        return per_device_general(stream, *rest)

    return jax.shard_map(
        step,
        mesh=mesh,
        in_specs=(
            P("groups", "out"),
            P(),
            P(None, "out"),
            P(None, "out"),
            P("out", None),
            P(("groups", "out")),
            P(("groups", "out"), None, None),
            P(("groups", "out"), None, None),
            P(("groups", "out"), None, None),
            P(("groups", "out"), None, None),
        ),
        out_specs=P("groups", "out"),
        check_vma=False,
    )
```

```python
import math

import jax
import jax.numpy as jnp
from jax import lax
from jax.experimental import pallas as pl
from jax.experimental.pallas import tpu as pltpu
from jax.sharding import PartitionSpec as P


HQ = 48
KVH = 4
HD = 128


rope_base = 1000000.0
norm_eps = 1e-05


def rotate(vec, position):
    half = vec.shape[-1] // 2
    index = jnp.arange(half, dtype=jnp.float32)
    freq = jnp.exp(index * (-2.0 * math.log(rope_base) / vec.shape[-1]))
    angle = position * freq
    cosine = jnp.cos(angle)
    sine = jnp.sin(angle)
    first = vec[..., :half]
    second = vec[..., half:]
    return jnp.concatenate(
        [first * cosine - second * sine, second * cosine + first * sine], axis=-1
    )


def dequant(cache, scales):
    rows, span, width = cache.shape
    blocks = scales.shape[1]
    factor = jnp.exp2(scales.astype(jnp.float32)).astype(jnp.bfloat16)
    shaped = cache.reshape(rows, blocks, span // blocks, KVH, width // KVH)
    return (shaped * factor[:, :, None, :, None]).reshape(rows, span, KVH, width // KVH)


def per_device_general(
    stream,
    norm_gain,
    w_query,
    w_keyval,
    w_out,
    lengths,
    key_cache,
    value_cache,
    key_scales,
    value_scales,
):
    local_rows = lengths.shape[0]
    xf = stream.astype(jnp.float32)
    whole = lax.all_gather(stream, "out", axis=1, tiled=True).astype(jnp.float32)
    meansq = jnp.mean(whole * whole, axis=-1, keepdims=True)
    normed = (whole * lax.rsqrt(meansq + norm_eps) * norm_gain).astype(jnp.bfloat16)
    q_local = jnp.dot(normed, w_query, preferred_element_type=jnp.float32).astype(jnp.bfloat16)
    kv_local = jnp.dot(normed, w_keyval, preferred_element_type=jnp.float32).astype(jnp.bfloat16)
    q_rows, kv_rows = (
        lax.all_to_all(q_local, "out", split_axis=0, concat_axis=1, tiled=True),
        lax.all_to_all(kv_local, "out", split_axis=0, concat_axis=1, tiled=True),
    )
    position = lengths.astype(jnp.float32)[:, None, None]
    rotated = rotate(q_rows.astype(jnp.float32).reshape(local_rows, HQ, HD), position).astype(
        jnp.bfloat16
    )
    rotated = rotated.reshape(local_rows, KVH, HQ // KVH, HD)
    new_key = rotate(
        kv_rows[:, : KVH * HD].astype(jnp.float32).reshape(local_rows, KVH, HD), position
    ).astype(jnp.bfloat16)
    new_value = kv_rows[:, KVH * HD :].reshape(local_rows, KVH, HD)
    factor = HD ** (-0.5)
    own = jnp.einsum("rkgd,rkd->rkg", rotated, new_key, preferred_element_type=jnp.float32) * factor
    span = key_cache.shape[1]
    scores = (
        jnp.einsum(
            "rkgd,rjkd->rkgj",
            rotated,
            dequant(key_cache, key_scales),
            preferred_element_type=jnp.float32,
        )
        * factor
    )
    valid = jnp.arange(span, dtype=jnp.int32)[None, :] < lengths[:, None]
    scores = jnp.where(valid[:, None, None, :], scores, -jnp.inf)
    top = jnp.maximum(jnp.max(scores, axis=-1), own)
    weights = jnp.exp(scores - top[..., None])
    own_weight = jnp.exp(own - top)
    total = jnp.sum(weights, axis=-1) + own_weight
    own_rounded = lax.optimization_barrier(own_weight.astype(jnp.bfloat16)).astype(jnp.float32)
    summed = jnp.einsum(
        "rkgj,rjkd->rkgd",
        weights.astype(jnp.bfloat16),
        dequant(value_cache, value_scales),
        preferred_element_type=jnp.float32,
    )
    summed = summed + own_rounded[..., None] * new_value.astype(jnp.float32)[:, :, None, :]
    attended = (summed / total[..., None]).astype(jnp.bfloat16).reshape(local_rows, HQ * HD)
    heads = lax.all_to_all(attended, "out", split_axis=1, concat_axis=0, tiled=True)
    partial_terms = jnp.dot(heads, w_out, preferred_element_type=jnp.float32)
    projected = lax.psum_scatter(partial_terms, "out", scatter_dimension=1, tiled=True)
    return (xf + projected).astype(jnp.bfloat16)


def swapped(value, mask, size):
    return lax.ppermute(value, "out", [(i, i ^ mask) for i in range(size)])


def room_kernel(out_ref):
    pass


def stage_kernel(*refs):
    refs[-1][...] = jnp.zeros_like(refs[-1])


def stage(cover):
    vmem = pl.BlockSpec(memory_space=pltpu.VMEM)
    small = pltpu.CompilerParams(vmem_limit_bytes=2 * 1024 * 1024)
    room = pl.pallas_call(
        room_kernel,
        out_shape=jax.ShapeDtypeStruct((2048, 512), jnp.bfloat16),
        out_specs=vmem,
        compiler_params=small,
        name="room",
    )()
    count = -(-cover // (2 * room.size))
    return pl.pallas_call(
        stage_kernel,
        out_shape=jax.ShapeDtypeStruct((8, 128), jnp.float32),
        in_specs=[pl.BlockSpec(memory_space=pl.ANY)] * count,
        out_specs=vmem,
        compiler_params=small,
        name="stage",
    )(*[room] * count)


def squares(refs):
    total = jnp.zeros((refs[0].shape[0], 128), jnp.float32)
    for ref in refs:
        part = ref[...].astype(jnp.float32)
        part = part * part
        for lane in range(0, part.shape[1], 128):
            total += part[:, lane : lane + 128]
    return total


def early_squares_kernel(*refs):
    refs[-1][...] = squares(refs[:-1])


def early_squares(shards):
    vmem = pl.BlockSpec(memory_space=pltpu.VMEM)
    return pl.pallas_call(
        early_squares_kernel,
        out_shape=jax.ShapeDtypeStruct((shards[0].shape[0], 128), jnp.float32),
        in_specs=[vmem] * len(shards),
        out_specs=vmem,
        compiler_params=pltpu.CompilerParams(vmem_limit_bytes=2 * 1024 * 1024),
        name="early_squares",
    )(*shards)


def project_kernel(order, pieces, late, *refs):
    shards = refs[:pieces]
    gain_ref, wq_ref, wkv_ref, _, early_ref, out_ref = refs[pieces:]
    rows, depth = shards[0].shape
    columns, kv_columns = wq_ref.shape[1], wkv_ref.shape[0]
    targets, per_target, _ = out_ref.shape
    me = lax.axis_index("out")
    square = early_ref[...] + squares([shards[k] for k in late])
    meansq = jnp.sum(square, axis=-1, keepdims=True) / (depth * pieces)
    inverse = lax.rsqrt(meansq + norm_eps)
    q_sum = jnp.zeros((rows, columns), jnp.float32)
    kv_sum = jnp.zeros((rows, kv_columns), jnp.float32)
    for k in range(pieces):
        start = pl.multiple_of(lax.bitwise_xor(me, order[k]) * depth, 128)
        gain = gain_ref[:, pl.ds(start, depth)]
        normed = (shards[k][...].astype(jnp.float32) * inverse * gain).astype(jnp.bfloat16)
        kv_sum += lax.dot_general(
            normed,
            wkv_ref[:, pl.ds(start, depth)],
            (((1,), (1,)), ((), ())),
            preferred_element_type=jnp.float32,
        )
        q_sum += jnp.dot(normed, wq_ref[pl.ds(start, depth), :], preferred_element_type=jnp.float32)
    odd = lax.bitwise_and(me, 1).astype(jnp.float32)
    both = jnp.concatenate([kv_sum * (1.0 - odd), kv_sum * odd], axis=-1)
    for k in range(targets):
        take = slice(k * per_target, (k + 1) * per_target)
        out_ref[k, :, :columns] = q_sum[take].astype(jnp.bfloat16)
        out_ref[k, :, columns:] = both[take].astype(jnp.bfloat16)


def project(order, late, shards, early, norm_gain, w_query, w_keyval, mark, per_target):
    pieces = len(shards)
    rows = shards[0].shape[0]
    vmem = pl.BlockSpec(memory_space=pltpu.VMEM)
    return pl.pallas_call(
        lambda *refs: project_kernel(order, pieces, late, *refs),
        out_shape=jax.ShapeDtypeStruct(
            (rows // per_target, per_target, w_query.shape[1] + 2 * w_keyval.shape[0]), jnp.bfloat16
        ),
        in_specs=[vmem] * (pieces + 5),
        out_specs=vmem,
        compiler_params=pltpu.CompilerParams(vmem_limit_bytes=16 * 1024 * 1024),
        name="project",
    )(*shards, norm_gain, w_query, w_keyval, mark, early)


def attend_kernel(
    lengths_ref, rows_ref, cos_ref, sin_ref, kf_ref, vf_ref, keys_ref, values_ref, out_ref
):
    sources, local_rows, _ = rows_ref.shape
    span = keys_ref.shape[1]
    each = out_ref.shape[-1] // HD
    heads = each * sources
    per_key = HQ // KVH // each
    blocks = kf_ref.shape[1]
    per_block = span // blocks
    each_row = range(local_rows)
    key_head = lax.broadcasted_iota(jnp.int32, (heads, HD), 0) % sources // per_key
    block_head = lax.broadcasted_iota(jnp.int32, (sources, per_block), 0) // per_key
    pick_row = lax.broadcasted_iota(jnp.int32, (2 * sources, sources), 0)
    pick_col = lax.broadcasted_iota(jnp.int32, (2 * sources, sources), 1)
    wanted = (pick_row % sources) // per_key + KVH * (pick_row // sources)
    pick = (pick_col // 2 == wanted).astype(jnp.bfloat16)
    place = lax.broadcasted_iota(jnp.int32, (heads, span), 1)

    def scaled(values, scale_ref, r):
        parts = []
        for b in range(blocks):
            scale = jnp.full((sources, per_block), scale_ref[r, b, 0])
            for k in range(1, KVH):
                scale = jnp.where(block_head == k, scale_ref[r, b, k], scale)
            scale = jnp.concatenate([scale] * each, axis=0)
            parts.append(values[:, b * per_block : (b + 1) * per_block] * scale)
        return jnp.concatenate(parts, axis=1)

    def turn(vec, r):
        cosine, sine = cos_ref[r : r + 1, :], sin_ref[r : r + 1, :]
        turned = vec * cosine + pltpu.roll(vec, HD // 2, 1) * sine
        return turned.astype(jnp.bfloat16).astype(jnp.float32)

    got = [rows_ref[:, r, :].astype(jnp.float32) for r in each_row]
    fresh = jnp.dot(
        pick,
        jnp.concatenate([g[:, each * HD :] for g in got], axis=1).astype(jnp.bfloat16),
        preferred_element_type=jnp.float32,
    )
    query, scores = [], []
    for r in each_row:
        query.append(
            turn(
                jnp.concatenate([got[r][:, g * HD : (g + 1) * HD] for g in range(each)], axis=0), r
            )
        )
        wide = jnp.concatenate(
            [jnp.where(key_head == k, query[r], 0.0) for k in range(KVH)], axis=1
        ).astype(jnp.bfloat16)
        scores.append(
            lax.dot_general(
                wide, keys_ref[r], (((1,), (1,)), ((), ())), preferred_element_type=jnp.float32
            )
        )
    own_weight, total, summed = [], [], []
    for r in each_row:
        new_key = turn(fresh[:sources, r * HD : (r + 1) * HD], r)
        new_key = jnp.concatenate([new_key] * each, axis=0)
        own = jnp.sum(query[r] * new_key, axis=-1, keepdims=True) * HD ** (-0.5)
        score = scaled(scores[r], kf_ref, r) * HD ** (-0.5)
        score = jnp.where(place < lengths_ref[r], score, -jnp.inf)
        top = jnp.maximum(jnp.max(score, axis=-1, keepdims=True), own)
        weights = jnp.exp(score - top)
        own_weight.append(jnp.exp(own - top))
        total.append(jnp.sum(weights, axis=-1, keepdims=True) + own_weight[r])
        rounded = scaled(weights.astype(jnp.bfloat16).astype(jnp.float32), vf_ref, r)
        summed.append(
            jnp.dot(
                rounded.astype(jnp.bfloat16), values_ref[r], preferred_element_type=jnp.float32
            )
        )
    for r in each_row:
        mine = summed[r][:, :HD]
        for k in range(1, KVH):
            mine = jnp.where(key_head == k, summed[r][:, k * HD : (k + 1) * HD], mine)
        new_value = jnp.concatenate([fresh[sources:, r * HD : (r + 1) * HD]] * each, axis=0)
        mine = mine + own_weight[r].astype(jnp.bfloat16).astype(jnp.float32) * new_value
        mine = (mine / total[r]).astype(jnp.bfloat16)
        for g in range(each):
            out_ref[:, r, g * HD : (g + 1) * HD] = mine[g * sources : (g + 1) * sources]


def attend(rows, columns, lengths, cosine, sine, key_factors, value_factors, key_cache, value_cache):
    sources, local_rows, _ = rows.shape
    smem = pl.BlockSpec(memory_space=pltpu.SMEM)
    vmem = pl.BlockSpec(memory_space=pltpu.VMEM)
    return pl.pallas_call(
        attend_kernel,
        out_shape=jax.ShapeDtypeStruct((sources, local_rows, columns), jnp.bfloat16),
        in_specs=[smem] + [vmem] * 3 + [smem] * 2 + [vmem] * 2,
        out_specs=vmem,
        compiler_params=pltpu.CompilerParams(vmem_limit_bytes=8 * 1024 * 1024),
        name="attend",
    )(lengths, rows, cosine, sine, key_factors, value_factors, key_cache, value_cache)


def expand_kernel(order, heads_ref, w_ref, out_ref):
    width = out_ref.shape[-1]
    me = lax.axis_index("out")
    heads = jnp.concatenate(
        [heads_ref[k].astype(jnp.float32) for k in range(heads_ref.shape[0])], axis=0
    ).astype(jnp.bfloat16)
    for k in range(len(order)):
        start = pl.multiple_of(lax.bitwise_xor(me, order[k]) * width, 128)
        out_ref[k] = jnp.dot(
            heads, w_ref[:, pl.ds(start, width)], preferred_element_type=jnp.float32
        ).astype(out_ref.dtype)


def expand(order, heads, w_out, width, dtype):
    vmem = pl.BlockSpec(memory_space=pltpu.VMEM)
    return pl.pallas_call(
        lambda *refs: expand_kernel(order, *refs),
        out_shape=jax.ShapeDtypeStruct(
            (len(order), heads.shape[0] * heads.shape[1], width), dtype
        ),
        in_specs=[vmem, vmem],
        out_specs=vmem,
        compiler_params=pltpu.CompilerParams(vmem_limit_bytes=16 * 1024 * 1024),
        name="expand",
    )(heads, w_out)


def per_device(
    size,
    stream,
    norm_gain,
    w_query,
    w_keyval,
    w_out,
    lengths,
    key_cache,
    value_cache,
    key_scales,
    value_scales,
):
    local_rows = lengths.shape[0]
    width = stream.shape[1]
    columns = w_query.shape[1]

    block = [m for m in (2, 4, 6) if m < size]
    tops = [1 << k for k in range(3, size.bit_length() - 1)]
    w_keyval = w_keyval.T
    norm_gain = norm_gain.reshape(1, -1)
    held = {0: stream}
    for bit in tops[::-1]:
        for mask in list(held):
            held[mask | bit] = swapped(held[mask], bit, size)
    last = max(held)
    held[last], mark = lax.optimization_barrier(
        (held[last], stage(2 * (w_query.size + w_keyval.size + w_out.size)))
    )
    for mask in list(held):
        for over in block:
            held[mask | over] = swapped(held[mask], over, size)
    for mask in list(held):
        held[mask | 1] = swapped(held[mask], 1, size)
    order = list(held)
    freq = jnp.exp(
        jnp.arange(HD // 2, dtype=jnp.float32) * (-2.0 * math.log(rope_base) / HD)
    )
    angle = lengths.astype(jnp.float32)[:, None] * freq
    cosine, sine = jnp.cos(angle), jnp.sin(angle)
    side = (
        jnp.concatenate([cosine, cosine], axis=-1),
        jnp.concatenate([-sine, sine], axis=-1),
        jnp.exp2(key_scales.astype(jnp.float32)),
        jnp.exp2(value_scales.astype(jnp.float32)),
    )
    side, held[size - 1] = lax.optimization_barrier((side, held[size - 1]))
    late = [k for k, m in enumerate(order) if m > size // 2 and m & 1]
    early = early_squares([held[m] for k, m in enumerate(order) if k not in late])
    shards = [held[m] for m in order]
    qkv = project(order, late, shards, early, norm_gain, w_query, w_keyval, mark, local_rows)
    rows = lax.all_to_all(qkv, "out", split_axis=0, concat_axis=0, tiled=True)
    attended = attend(rows, columns, lengths, *side, key_cache, value_cache)
    heads = lax.all_to_all(attended, "out", split_axis=0, concat_axis=0, tiled=True)

    owed = {}
    spans = [t for t in range(0, size, 8)][::-1]
    for top in spans:
        near = [top | m for m in block + [0]]
        away = [m | 1 for m in near]
        sent = expand(away, heads, w_out, width, jnp.bfloat16)
        sent = swapped(sent, 1, size)
        kept = expand(near, heads, w_out, width, jnp.float32)
        for k, mask in enumerate(near):
            owed[mask] = kept[k] + sent[k].astype(jnp.float32)
        for mask in near[-2::-1]:
            got = swapped(owed[mask].astype(jnp.bfloat16), mask ^ top, size)
            owed[top] = owed[top] + got.astype(jnp.float32)
    for bit in tops[::-1]:
        for mask in [m for m in spans if m & bit and m < 2 * bit]:
            got = swapped(owed[mask].astype(jnp.bfloat16), bit, size)
            owed[mask ^ bit] = owed[mask ^ bit] + got.astype(jnp.float32)
    return (stream.astype(jnp.float32) + owed[0]).astype(jnp.bfloat16)


def solution(mesh):
    size = mesh.shape["out"]

    def step(stream, *rest):
        columns = rest[1].shape[1]
        whole_heads = columns % HD == 0 and HQ // KVH * HD % columns == 0 and 2 * rest[2].shape[1] == HD
        if size & (size - 1) == 0 and stream.shape[1] % 128 == 0 and whole_heads:
            return per_device(size, stream, *rest)
        return per_device_general(stream, *rest)

    return jax.shard_map(
        step,
        mesh=mesh,
        in_specs=(
            P("groups", "out"),
            P(),
            P(None, "out"),
            P(None, "out"),
            P("out", None),
            P(("groups", "out")),
            P(("groups", "out"), None, None),
            P(("groups", "out"), None, None),
            P(("groups", "out"), None, None),
            P(("groups", "out"), None, None),
        ),
        out_specs=P("groups", "out"),
        check_vma=False,
    )
```
